256 devices in a mesh: dp: 32 (over z, x_hi, core), tensor: 8 (over y, x_lo).
Axes of the slice: x: 4 (x_hi: 2, x_lo: 2; x = x_hi * 2 + x_lo), y: 4, z: 8, core: 2. Of those that a mesh axis runs over, the one named last changes fastest.
Arguments:
- context: bfloat16 [12288, 8192], P('dp', 'tensor'), may hold values from -6 to 6
- output_weight: bfloat16 [8192, 8192], P('tensor', 'dp'), may hold values from -0.0625 to 0.0625
- adapter_down_weight: bfloat16 [8192, 16], P('tensor'), may hold values from -0.0625 to 0.0625
- adapter_up_weight: bfloat16 [16, 8192], replicated, may hold values from -0.29882812 to 0.29882812
- residual: bfloat16 [12288, 8192], P('dp', 'tensor'), may hold values from -60 to 60
- frozen_residual_delta: bfloat16 [12288, 8192], P('dp', 'tensor'), may hold values from -6 to 6
- harmful_count: int32 [32], replicated, may hold values from 48 to 192
- retain_count: int32 [32], replicated, may hold values from 48 to 192
Outputs:
- adapted: bfloat16 [12288, 8192], P('dp', 'tensor')
- grad_a: float32 [8192, 16], P('tensor')
- grad_b: float32 [16, 8192], replicated
The draws below stay inside these ranges and needn't reach their ends.
All inputs are finite; a program needn't handle non-finite values.
Results may differ from the reference program's by a relative error of at most 0.005.
Values may be sent and summed in bfloat16 or wider, within the bound.
A program may use at most 128 MiB of HBM per device.

```python
import math
import jax
import jax.numpy as jnp
from jax import lax

MODEL_WIDTH = 8192
ADAPTER_RANK = 16
LEN = 384
CONTEXT_WIDTH = 8192
TOKENS = 12288
N_DP = 32


def draw_residual(key, part):
    key_scale, key_base = jax.random.split(jax.random.fold_in(key, 11))
    row_scale = jnp.exp(jax.random.uniform(key_scale, (TOKENS, 1), jnp.float32, 0.0, math.log(10.0)))
    base = jnp.clip(jax.random.normal(key_base, (TOKENS, MODEL_WIDTH), jnp.float32), -6.0, 6.0)
    return (row_scale * base).astype(jnp.bfloat16)


def place_ends(entries, stream_key, least, high):
    shape = entries.shape
    spot = [jax.random.randint(jax.random.fold_in(stream_key, axis), (), 0, shape[axis]) for axis in range(len(shape))]
    entries = entries.at[tuple(spot)].set(least)
    longest = shape.index(max(shape))
    spot[longest] = (spot[longest] + 1) % shape[longest]
    return entries.at[tuple(spot)].set(high)


def steps_of(rng, extent, cuts, low, largest):
    def one(axis_at, parts):
        steps = jax.random.uniform(jax.random.fold_in(jax.random.fold_in(rng, 6), axis_at), (parts,), jnp.float32, low / len(cuts), largest / len(cuts))
        return jnp.repeat(jnp.exp(steps), extent[axis_at] // parts).reshape((-1,) + (1,) * (len(extent) - axis_at - 1))

    loudness = one(*cuts[0])
    for cut in cuts[1:]:
        loudness = loudness * one(*cut)
    return loudness


def bell_draw(key, dims, spread, limit, cuts=(), held_as=jnp.bfloat16):
    drawn = jax.random.normal(key, dims, jnp.float32) * spread
    if len(cuts) > 0:
        drawn = steps_of(key, dims, cuts, -0.22, 0.18) * drawn
    return jnp.clip(drawn, min=-limit, max=limit).astype(held_as)


def setup_inputs(seed: int = 0) -> dict:
    streams_of = jax.random.split(jax.random.key(seed), 9)
    return {
        "context": bell_draw(streams_of[0], (TOKENS, CONTEXT_WIDTH), 1.0, 6.0, ((0, 32), (1, 8))),
        "output_weight": bell_draw(streams_of[1], (CONTEXT_WIDTH, MODEL_WIDTH), CONTEXT_WIDTH ** -0.5, 0.0625, ((0, 8), (1, 32))),
        "adapter_down_weight": bell_draw(streams_of[2], (CONTEXT_WIDTH, ADAPTER_RANK), CONTEXT_WIDTH ** -0.5, 0.0625, ((0, 8),)),
        "adapter_up_weight": bell_draw(streams_of[3], (ADAPTER_RANK, MODEL_WIDTH), 0.05, 0.29882812),
        "residual": draw_residual(jax.random.fold_in(streams_of[8], 71), 0),
        "frozen_residual_delta": bell_draw(streams_of[5], (TOKENS, MODEL_WIDTH), 1.0, 6.0, ((0, 32), (1, 8))),
        "harmful_count": place_ends(jax.random.randint(streams_of[6], (N_DP,), LEN // 8, LEN // 2 + 1), jax.random.fold_in(streams_of[6], 1), LEN // 8, (LEN // 2 + 1) - 1).astype(jnp.int32),
        "retain_count": place_ends(jax.random.randint(streams_of[7], (N_DP,), LEN // 8, LEN // 2 + 1), jax.random.fold_in(streams_of[7], 1), LEN // 8, (LEN // 2 + 1) - 1).astype(jnp.int32),
    }


ADAPTER_SCALE = 2.0
NORM_EPS = 1e-06
REROUTE_WEIGHT = 65536.0
RETAIN_WEIGHT = 1024.0

def row_gradient(hidden_states, target, sq_state, sq_target, cross_term, gap_sq, harmful, retained, harm_total, keep_total):
    norm_h = jnp.sqrt(sq_state + NORM_EPS)
    norm_g = jnp.sqrt(sq_target + NORM_EPS)
    cosine = cross_term / (norm_h * norm_g)
    distance = jnp.sqrt(gap_sq + NORM_EPS)
    weight_harm = REROUTE_WEIGHT / harm_total * harmful
    weight_keep = RETAIN_WEIGHT / keep_total * retained
    first = (weight_harm / (norm_h * norm_g))[:, None] * target
    second = (weight_harm * cosine / (norm_h * norm_h))[:, None] * hidden_states
    third = (weight_keep / distance)[:, None] * (hidden_states - target)
    return first - second + third

def reference(context, output_weight, adapter_down_weight, adapter_up_weight, residual, frozen_residual_delta, harmful_count, retain_count):
    harm_total = jnp.sum(harmful_count).astype(jnp.float32)
    keep_total = jnp.sum(retain_count).astype(jnp.float32)
    up_weight_single = adapter_up_weight.astype(jnp.float32)
    ctx_all = context.reshape(N_DP, LEN, CONTEXT_WIDTH)
    res_all = residual.reshape(N_DP, LEN, MODEL_WIDTH)
    fro_all = frozen_residual_delta.reshape(N_DP, LEN, MODEL_WIDTH)
    positions = jnp.arange(LEN, dtype=jnp.int32)

    def per_sequence(carry, items):
        acc_a, up_gradient_total = carry
        context_rows, residual_rows, fro_rows, harm_here, keep_here = items
        attention_output = jnp.dot(context_rows, output_weight, preferred_element_type=jnp.float32)
        reduced_state = jnp.dot(context_rows, adapter_down_weight, preferred_element_type=jnp.float32)
        hidden_states = residual_rows.astype(jnp.float32) + attention_output + ADAPTER_SCALE * jnp.dot(reduced_state, up_weight_single, precision=lax.Precision.HIGHEST)
        target = residual_rows.astype(jnp.float32) + fro_rows.astype(jnp.float32)
        harmful = (positions < harm_here).astype(jnp.float32)
        retained = ((positions >= harm_here) & (positions < harm_here + keep_here)).astype(jnp.float32)
        gap = hidden_states - target
        output_gradient = row_gradient(hidden_states, target, lax.optimization_barrier(jnp.sum(hidden_states * hidden_states, axis=1)), lax.optimization_barrier(jnp.sum(target * target, axis=1)), lax.optimization_barrier(jnp.sum(hidden_states * target, axis=1)), lax.optimization_barrier(jnp.sum(gap * gap, axis=1)), harmful, retained, harm_total, keep_total)
        reduced_gradient = ADAPTER_SCALE * jnp.dot(output_gradient, up_weight_single.T, precision=lax.Precision.HIGHEST)
        acc_a = acc_a + jnp.dot(context_rows.astype(jnp.float32).T, reduced_gradient, precision=lax.Precision.HIGHEST)
        up_gradient_total = up_gradient_total + ADAPTER_SCALE * jnp.dot(reduced_state.T, output_gradient, precision=lax.Precision.HIGHEST)
        return ((acc_a, up_gradient_total), hidden_states.astype(jnp.bfloat16))
    start = (jnp.zeros((CONTEXT_WIDTH, ADAPTER_RANK), jnp.float32), jnp.zeros((ADAPTER_RANK, MODEL_WIDTH), jnp.float32))
    (grad_a, grad_b), adapted = lax.scan(per_sequence, start, (ctx_all, res_all, fro_all, harmful_count, retain_count))
    return (adapted.reshape(TOKENS, MODEL_WIDTH), grad_a, grad_b)
```

```python
import jax
import jax.numpy as jnp
from jax import lax
from jax.experimental import pallas as pl
from jax.experimental.pallas import tpu as pltpu
from jax.sharding import PartitionSpec as P

NORM_EPS = 1e-06
REROUTE_WEIGHT = 65536.0
RETAIN_WEIGHT = 1024.0

NZ = 8
NY = 4
NX = 4
NT = 8
NDP = 32
LEN = 384
HALF = LEN // 2
KB = 1024
RANK = 16
F32 = jnp.float32
BF16 = jnp.bfloat16
NT_DIMS = (((1,), (1,)), ((), ()))
TN_DIMS = (((0,), (0,)), ((), ()))
NN_DIMS = (((1,), (0,)), ((), ()))


def split3(value):
    hi = value.astype(BF16)
    rest = value - hi.astype(F32)
    mid = rest.astype(BF16)
    low = (rest - mid.astype(F32)).astype(BF16)
    return jnp.concatenate([hi, mid, low], axis=0)


def fold3(value):
    return value[0:RANK] + value[RANK : 2 * RANK] + value[2 * RANK : 3 * RANK]


def dot32(a, b, dims):
    return lax.dot_general(a, b, dims, preferred_element_type=F32)


def dot_high(a, b, dims):
    return lax.dot_general(a, b, dims, precision=lax.Precision.HIGHEST, preferred_element_type=F32)


def kernel(
    ctx_hbm,
    w_hbm,
    down_ref,
    up_hbm,
    res_hbm,
    dlt_hbm,
    harm_ref,
    keep_ref,
    adapted_hbm,
    ga_ref,
    gb_ref,
    a_buf,
    w_buf,
    p_buf,
    r_buf,
    xs_buf,
    xr_buf,
    up_buf,
    res_buf,
    dlt_buf,
    ad_buf,
    ghi_buf,
    glo_buf,
    early_send,
    early_recv,
    late_send,
    late_recv,
    g_send,
    g_recv,
    h_send,
    h_recv,
    b_recv,
    acc_buf,
    in_sem,
    out_sem,
    a_send,
    a_sem,
    w_send,
    w_sem,
    p_send,
    r_sem,
    x_send,
    x_sem,
    small_send,
    early_sem,
    late_sem,
    g_sem,
    h_sem,
    b_sem,
):
    dp = lax.axis_index("dp")
    t = lax.axis_index("tensor")
    z = dp // 4
    xh = (dp // 2) % 2
    c = dp % 2
    y = t // 2
    xl = t % 2
    x = 2 * xh + xl
    right = (x + 1) % NX
    left = (x + 3) % NX

    def dev(z_to, y_to, x_to, c_to):
        return (z_to * 4 + (x_to // 2) * 2 + c_to, y_to * 2 + x_to % 2)

    def remote(src, dst, send, recv, to):
        return pltpu.make_async_remote_copy(
            src_ref=src,
            dst_ref=dst,
            send_sem=send,
            recv_sem=recv,
            device_id=to,
            device_id_type=pl.DeviceIdType.MESH,
        )

    def wait_copy(ref, sem):
        pltpu.make_async_copy(ref, ref, sem).wait()

    def wait_all(ref, sems, count):
        @pl.loop(0, count)
        def _(source):
            wait_copy(ref.at[source], sems.at[source])

    to_right = dev(z, y, right, c)
    to_left = dev(z, y, left, c)
    to_core = dev(z, y, x, 1 - c)
    to_pair = dev(z, y, 2 * xh + (1 - xl), c)
    to_up = dev((z + 1) % NZ, y, x, c)
    to_down = dev((z + 7) % NZ, y, x, c)

    def a_index(x_of, c_of):
        return (x_of % 2) * 4 + (x_of // 2) * 2 + c_of

    own = a_index(x, c)
    own_a = pltpu.make_async_copy(ctx_hbm, a_buf.at[own], in_sem.at[0])
    own_a.start()
    own_w = pltpu.make_async_copy(
        w_hbm.at[:, pl.ds(pl.multiple_of(xl * 128, 128), 128)], w_buf.at[xl], w_sem.at[0]
    )
    own_w.start()
    load_up = pltpu.make_async_copy(
        up_hbm.at[:, pl.ds(pl.multiple_of(t * KB, KB), KB)], up_buf, in_sem.at[1]
    )
    load_up.start()
    load_res = pltpu.make_async_copy(res_hbm, res_buf, in_sem.at[2])
    load_res.start()
    load_dlt = pltpu.make_async_copy(dlt_hbm, dlt_buf, in_sem.at[3])
    load_dlt.start()

    barrier = pltpu.get_barrier_semaphore()

    def greet(to):
        pl.semaphore_signal(barrier, inc=1, device_id=to, device_id_type=pl.DeviceIdType.MESH)

    for step in range(1, NY):
        greet(dev(z, (y + step) % NY, x, 1 - c))
    greet(dev(z, y, 2 * (1 - xh) + (1 - xl), c))
    for step in range(1, NT):
        greet((dp, (t + step) % NT))

    @pl.loop(1, NDP)
    def _(step):
        greet(((dp + step) % NDP, t))

    pl.semaphore_wait(barrier, (NY - 1) + 1 + (NT - 1) + (NDP - 1))

    send_pair = remote(
        w_hbm.at[:, pl.ds(pl.multiple_of((1 - xl) * 128, 128), 128)],
        w_buf.at[xl],
        w_send,
        w_sem.at[1],
        to_pair,
    )
    send_pair.start()

    def send_a_rows(block, rows, sem, to):
        return remote(
            a_buf.at[block, pl.ds(rows * HALF, HALF)],
            a_buf.at[block, pl.ds(rows * HALF, HALF)],
            a_send,
            a_sem.at[sem],
            to,
        )

    def send_a_block(block, sem, to):
        return remote(a_buf.at[block], a_buf.at[block], a_send, a_sem.at[sem], to)

    def wait_a_rows(block, rows, sem):
        ref = a_buf.at[block, pl.ds(rows * HALF, HALF)]
        pltpu.make_async_copy(ref, ref, a_sem.at[sem]).wait()

    def wait_a_block(block, sem):
        ref = a_buf.at[block]
        pltpu.make_async_copy(ref, ref, a_sem.at[sem]).wait()

    own_a.wait()
    send_a_rows(own, 0, 1, to_right).start()
    send_a_rows(own, 1, 4, to_left).start()
    send_a_rows(own, 1, 2, to_right).start()
    send_a_rows(own, 0, 3, to_left).start()
    send_a_block(own, 0, to_core).start()

    def wait_w(slot, part):
        ref = w_buf.at[slot * 2 + (xl + part) % 2]
        pltpu.make_async_copy(ref, ref, w_sem.at[slot * 2 + part]).wait()

    def send_w(slot, part, to_slot, to):
        row = (xl + part) % 2
        remote(
            w_buf.at[slot * 2 + row],
            w_buf.at[to_slot * 2 + row],
            w_send,
            w_sem.at[to_slot * 2 + part],
            to,
        ).start()

    wait_w(0, 0)
    send_w(0, 0, 1, to_up)
    send_w(0, 0, 2, to_down)

    load_up.wait()
    load_res.wait()
    load_dlt.wait()
    early_send[0:RANK] = dot32(down_ref[...], a_buf[own], NT_DIMS)
    early_send[RANK : 2 * RANK] = dot32(up_buf[...], res_buf[...], NT_DIMS) + dot32(
        up_buf[...], dlt_buf[...], NT_DIMS
    )
    ones = jnp.ones((8, 128), F32)
    acc_buf[0] = jnp.zeros((LEN, 128), F32)
    for j in range(8):
        cols = pl.ds(j * 128, 128)
        target = res_buf[:, cols].astype(F32) + dlt_buf[:, cols].astype(F32)
        acc_buf[0] += target * target
    early_send[2 * RANK :] = dot_high(ones, acc_buf[0], NT_DIMS)
    for step in range(1, NT):
        remote(
            early_send, early_recv.at[t], small_send.at[0], early_sem.at[t], (dp, (t + step) % NT)
        ).start()
    pltpu.make_async_copy(early_send, early_recv.at[t], early_sem.at[t]).start()

    wait_w(0, 1)
    send_w(0, 1, 1, to_up)
    send_w(0, 1, 2, to_down)

    def forward(slot, part, to_slot, to):
        wait_w(slot, part)
        send_w(slot, part, to_slot, to)

    def multiply(xh_of, slots):
        total = None
        for k in range(2):
            rows = a_buf[pl.ds(k * 4 + xh_of * 2, 2)].reshape(2 * LEN, KB)
            cols = [w_buf[slot * 2 + k] for slot in slots]
            cols = cols[0] if len(cols) == 1 else jnp.concatenate(cols, axis=1)
            part = dot32(rows, cols, NN_DIMS)
            total = part if total is None else total + part
        for i, slot in enumerate(slots):
            p_buf[pl.ds(slot * 4 + xh_of * 2, 2)] = (
                total[:, i * 128 : (i + 1) * 128].astype(BF16).reshape(2, LEN, 128)
            )
        offset = {0: 0, 1: 7, 2: 1, 3: 6, 4: 2, 5: 5, 6: 3, 7: 4}
        for slot in slots:
            owner = (z + offset[slot]) % NZ
            y_to = owner // 2
            group = (owner % 2) * 2 + xh_of
            for c_of in range(2):
                src = p_buf.at[slot * 4 + xh_of * 2 + c_of]
                dst = r_buf.at[group, y * 2 + c]
                here = (y_to == y) & (c_of == c)

                @pl.when(here)
                def _():
                    pltpu.make_async_copy(src, dst, r_sem.at[group, y * 2 + c]).start()

                @pl.when(jnp.logical_not(here))
                def _():
                    remote(
                        src, dst, p_send, r_sem.at[group, y * 2 + c], dev(z, y_to, x, c_of)
                    ).start()

    forward(1, 0, 3, to_up)
    forward(2, 0, 4, to_down)
    wait_a_rows(a_index(left, c), 0, 1)
    send_a_rows(a_index(left, c), 0, 5, to_right).start()
    wait_a_rows(a_index(right, c), 1, 4)
    send_a_rows(a_index(right, c), 1, 6, to_left).start()
    forward(1, 1, 3, to_up)
    forward(2, 1, 4, to_down)
    wait_a_rows(a_index(left, c), 1, 2)
    send_a_block(a_index(left, c), 7, to_core).start()
    wait_a_rows(a_index(right, c), 0, 3)
    send_a_block(a_index(right, c), 8, to_core).start()
    forward(3, 0, 5, to_up)
    forward(4, 0, 6, to_down)
    wait_a_block(a_index(x, 1 - c), 0)
    wait_a_block(a_index(left, 1 - c), 7)
    wait_a_block(a_index(right, 1 - c), 8)
    multiply(xh, (0,))
    multiply(xh, (1, 2))
    forward(3, 1, 5, to_up)
    forward(4, 1, 6, to_down)
    multiply(xh, (3, 4))
    wait_a_rows(a_index((x + 2) % NX, c), 0, 5)
    wait_a_rows(a_index((x + 2) % NX, c), 1, 6)
    send_a_block(a_index((x + 2) % NX, c), 9, to_core).start()
    forward(5, 0, 7, to_up)
    wait_w(6, 0)
    wait_a_block(a_index((x + 2) % NX, 1 - c), 9)
    multiply(1 - xh, (0,))
    multiply(1 - xh, (1, 2))
    multiply(1 - xh, (3, 4))
    wait_w(5, 1)
    forward(6, 1, 7, to_down)
    multiply(1 - xh, (5, 6))
    multiply(xh, (5, 6))
    wait_w(7, 0)
    wait_w(7, 1)
    multiply(1 - xh, (7,))
    multiply(xh, (7,))

    for xh_of in range(2):
        for xl_of in range(2):
            group = xl_of * 2 + xh_of
            x_to = xh_of * 2 + xl_of
            for source in range(8):
                wait_copy(r_buf.at[group, source], r_sem.at[group, source])
            for c_of in range(2):
                total = r_buf[group, c_of].astype(F32)
                for y_of in range(1, NY):
                    total = total + r_buf[group, y_of * 2 + c_of].astype(F32)
                xs_buf[x_to, c_of] = total.astype(BF16)

            @pl.when(x_to == x)
            def _():
                pltpu.make_async_copy(xs_buf.at[x_to], xr_buf.at[x], x_sem.at[x]).start()

            @pl.when(x_to != x)
            def _():
                remote(
                    xs_buf.at[x_to], xr_buf.at[x], x_send, x_sem.at[x], dev(z, y, x_to, c)
                ).start()

    wait_all(early_recv, early_sem, NT)
    early = early_recv[0]
    for other in range(1, NT):
        early = early + early_recv[other]
    low_rank = early[0:RANK]
    target_up = early[RANK : 2 * RANK]
    sq_target = early[2 * RANK : 2 * RANK + 1]
    low3 = split3(2.0 * low_rank)

    for source in range(NX):
        wait_copy(xr_buf.at[source], x_sem.at[source])
    for i in range(3):
        acc_buf[i] = jnp.zeros((LEN, 128), F32)
    for j in range(8):
        cols = pl.ds(j * 128, 128)
        x_of = (j // 4) * 2 + j % 2
        c_of = (j // 2) % 2
        up3 = jnp.concatenate([up_buf[:, cols]] * 3, axis=0)
        res = res_buf[:, cols].astype(F32)
        state = res + xr_buf[x_of, c_of].astype(F32) + dot32(low3, up3, TN_DIMS)
        ad_buf[:, cols] = state.astype(BF16)
        target = res + dlt_buf[:, cols].astype(F32)
        gap = state - target
        acc_buf[0] += state * state
        acc_buf[1] += state * target
        acc_buf[2] += gap * gap
        high = gap.astype(BF16)
        ghi_buf[:, cols] = high
        glo_buf[:, cols] = (gap - high.astype(F32)).astype(BF16)
    store_adapted = pltpu.make_async_copy(ad_buf, adapted_hbm, out_sem)
    store_adapted.start()
    late_send[0:RANK] = dot32(up_buf[...], ghi_buf[...], NT_DIMS) + dot32(
        up_buf[...], glo_buf[...], NT_DIMS
    )
    for i in range(3):
        late_send[RANK + 8 * i : RANK + 8 * i + 8] = dot_high(ones, acc_buf[i], NT_DIMS)
    for step in range(1, NT):
        remote(
            late_send, late_recv.at[t], small_send.at[1], late_sem.at[t], (dp, (t + step) % NT)
        ).start()
    pltpu.make_async_copy(late_send, late_recv.at[t], late_sem.at[t]).start()

    rank = lax.broadcasted_iota(jnp.int32, (1, NDP), 1)

    def total_and_here(count_ref):
        count = count_ref[...].astype(F32)
        here = jnp.where(rank == dp, count, 0.0)
        return jnp.sum(count, axis=1, keepdims=True), jnp.sum(here, axis=1, keepdims=True)

    harm_sum, harm_here = total_and_here(harm_ref)
    keep_sum, keep_here = total_and_here(keep_ref)
    position = lax.broadcasted_iota(jnp.int32, (1, LEN), 1).astype(F32)
    harmful = (position < harm_here).astype(F32)
    retained = ((position >= harm_here) & (position < harm_here + keep_here)).astype(F32)
    weight_harm = REROUTE_WEIGHT / harm_sum * harmful
    weight_keep = RETAIN_WEIGHT / keep_sum * retained

    wait_all(late_recv, late_sem, NT)
    late = late_recv[0]
    for other in range(1, NT):
        late = late + late_recv[other]
    gap_up = late[0:RANK]
    norm_h = jnp.sqrt(late[RANK : RANK + 1] + NORM_EPS)
    cross = late[RANK + 8 : RANK + 9]
    distance = jnp.sqrt(late[RANK + 16 : RANK + 17] + NORM_EPS)
    norm_g = jnp.sqrt(sq_target + NORM_EPS)
    cosine = cross / (norm_h * norm_g)
    first = weight_harm / (norm_h * norm_g)
    second = weight_harm * cosine / (norm_h * norm_h)
    third = weight_keep / distance
    by_target = 2.0 * (first - second)
    by_gap = 2.0 * (third - second)
    low_cot = by_target * target_up + by_gap * gap_up
    ga = fold3(dot32(split3(low_cot), a_buf[own], NN_DIMS))
    left_side = split3(low_rank * by_target)
    right_side = split3(low_rank * by_gap)
    gb = fold3(
        dot32(left_side, res_buf[...], NN_DIMS)
        + dot32(left_side, dlt_buf[...], NN_DIMS)
        + dot32(right_side, ghi_buf[...], NN_DIMS)
        + dot32(right_side, glo_buf[...], NN_DIMS)
    )
    for j in range(8):
        g_send[0:RANK, j, :] = ga[:, j * 128 : (j + 1) * 128]
        g_send[RANK:, j, :] = gb[:, j * 128 : (j + 1) * 128]

    @pl.loop(1, NDP)
    def _(step):
        to = (dp + step) % NDP
        remote(g_send.at[to], g_recv.at[dp], small_send.at[2], g_sem.at[dp], (to, t)).start()

    pltpu.make_async_copy(g_send.at[dp], g_recv.at[dp], g_sem.at[dp]).start()
    wait_all(g_recv, g_sem, NDP)
    total = g_recv[0]
    for other in range(1, NDP):
        total = total + g_recv[other]
    h_send[...] = total

    @pl.loop(1, NDP)
    def _(step):
        remote(
            h_send, h_recv.at[dp], small_send.at[3], h_sem.at[dp], ((dp + step) % NDP, t)
        ).start()

    pltpu.make_async_copy(h_send, h_recv.at[dp], h_sem.at[dp]).start()
    wait_all(h_recv, h_sem, NDP)
    gb_rows = h_recv.at[pl.ds(RANK, RANK)]
    for step in range(1, NT):
        remote(gb_rows, b_recv.at[t], small_send.at[4], b_sem.at[t], (dp, (t + step) % NT)).start()
    pltpu.make_async_copy(gb_rows, b_recv.at[t], b_sem.at[t]).start()
    for j in range(8):
        ga_ref[:, j * 128 : (j + 1) * 128] = h_recv[0:RANK, j, :]
    wait_all(b_recv, b_sem, NT)
    for t_of in range(NT):
        for j in range(8):
            start = t_of * KB + j * 128
            gb_ref[:, start : start + 128] = b_recv[t_of, :, j, :]

    wait_copy(a_buf.at[pl.ds(0, 7)], a_send)
    wait_copy(w_buf.at[pl.ds(0, 15)], w_send)
    wait_copy(p_buf.at[pl.ds(0, 28)], p_send)
    wait_copy(xs_buf.at[pl.ds(0, 3)], x_send)
    wait_copy(early_recv.at[pl.ds(0, NT - 1)], small_send.at[0])
    wait_copy(late_recv.at[pl.ds(0, NT - 1)], small_send.at[1])
    wait_copy(g_recv.at[pl.ds(0, NDP - 1)], small_send.at[2])
    wait_copy(h_recv.at[pl.ds(0, NDP - 1)], small_send.at[3])
    wait_copy(b_recv.at[pl.ds(0, NT - 1)], small_send.at[4])
    store_adapted.wait()


def local(ctx, w, down, up, res, dlt, harm, keep):
    vmem = pl.BlockSpec(memory_space=pltpu.VMEM)
    anyw = pl.BlockSpec(memory_space=pl.ANY)
    adapted, ga, gb = pl.pallas_call(
        kernel,
        out_shape=(
            jax.ShapeDtypeStruct((LEN, KB), BF16),
            jax.ShapeDtypeStruct((RANK, KB), F32),
            jax.ShapeDtypeStruct((RANK, NT * KB), F32),
        ),
        in_specs=[anyw, anyw, vmem, anyw, anyw, anyw, vmem, vmem],
        out_specs=(anyw, vmem, vmem),
        scratch_shapes=[
            pltpu.VMEM((8, LEN, KB), BF16),
            pltpu.VMEM((16, KB, 128), BF16),
            pltpu.VMEM((32, LEN, 128), BF16),
            pltpu.VMEM((4, 8, LEN, 128), BF16),
            pltpu.VMEM((4, 2, LEN, 128), BF16),
            pltpu.VMEM((4, 2, LEN, 128), BF16),
            pltpu.VMEM((RANK, KB), BF16),
            pltpu.VMEM((LEN, KB), BF16),
            pltpu.VMEM((LEN, KB), BF16),
            pltpu.VMEM((LEN, KB), BF16),
            pltpu.VMEM((LEN, KB), BF16),
            pltpu.VMEM((LEN, KB), BF16),
            pltpu.VMEM((40, LEN), F32),
            pltpu.VMEM((NT, 40, LEN), F32),
            pltpu.VMEM((40, LEN), F32),
            pltpu.VMEM((NT, 40, LEN), F32),
            pltpu.VMEM((NDP, 8, 128), F32),
            pltpu.VMEM((NDP, 8, 128), F32),
            pltpu.VMEM((8, 128), F32),
            pltpu.VMEM((NDP, 8, 128), F32),
            pltpu.VMEM((NT, RANK, 8, 128), F32),
            pltpu.VMEM((3, LEN, 128), F32),
            pltpu.SemaphoreType.DMA((4,)),
            pltpu.SemaphoreType.DMA,
            pltpu.SemaphoreType.DMA,
            pltpu.SemaphoreType.DMA((10,)),
            pltpu.SemaphoreType.DMA,
            pltpu.SemaphoreType.DMA((16,)),
            pltpu.SemaphoreType.DMA,
            pltpu.SemaphoreType.DMA((4, 8)),
            pltpu.SemaphoreType.DMA,
            pltpu.SemaphoreType.DMA((NX,)),
            pltpu.SemaphoreType.DMA((5,)),
            pltpu.SemaphoreType.DMA((NT,)),
            pltpu.SemaphoreType.DMA((NT,)),
            pltpu.SemaphoreType.DMA((NDP,)),
            pltpu.SemaphoreType.DMA((NDP,)),
            pltpu.SemaphoreType.DMA((NT,)),
        ],
        compiler_params=pltpu.CompilerParams(
            collective_id=0, has_side_effects=True, vmem_limit_bytes=56 * 1024 * 1024
        ),
    )(ctx, w, down.T, up, res, dlt, harm.reshape(1, NDP), keep.reshape(1, NDP))
    return adapted, ga.T, gb


def solution(mesh):
    return jax.shard_map(
        local,
        mesh=mesh,
        in_specs=(
            P("dp", "tensor"),
            P("tensor", "dp"),
            P("tensor", None),
            P(),
            P("dp", "tensor"),
            P("dp", "tensor"),
            P(),
            P(),
        ),
        out_specs=(P("dp", "tensor"), P("tensor", None), P()),
        check_vma=False,
    )
```

```python
import jax
import jax.numpy as jnp
from jax import lax
from jax.experimental import pallas as pl
from jax.experimental.pallas import tpu as pltpu
from jax.sharding import PartitionSpec as P

NORM_EPS = 1e-06
REROUTE_WEIGHT = 65536.0
RETAIN_WEIGHT = 1024.0

NZ = 8
NY = 4
NX = 4
NT = 8
NDP = 32
LEN = 384
HALF = LEN // 2
KB = 1024
RANK = 16
F32 = jnp.float32
BF16 = jnp.bfloat16
NT_DIMS = (((1,), (1,)), ((), ()))
TN_DIMS = (((0,), (0,)), ((), ()))
NN_DIMS = (((1,), (0,)), ((), ()))


def split3(value):
    hi = value.astype(BF16)
    rest = value - hi.astype(F32)
    mid = rest.astype(BF16)
    low = (rest - mid.astype(F32)).astype(BF16)
    return jnp.concatenate([hi, mid, low], axis=0)


def fold3(value):
    return value[0:RANK] + value[RANK : 2 * RANK] + value[2 * RANK : 3 * RANK]


def dot32(a, b, dims):
    return lax.dot_general(a, b, dims, preferred_element_type=F32)


def dot_high(a, b, dims):
    return lax.dot_general(a, b, dims, precision=lax.Precision.HIGHEST, preferred_element_type=F32)


def kernel(
    ctx_hbm,
    w_hbm,
    down_ref,
    up_hbm,
    res_hbm,
    dlt_hbm,
    harm_ref,
    keep_ref,
    adapted_hbm,
    ga_ref,
    gb_ref,
    a_buf,
    w_buf,
    p_buf,
    r_buf,
    f_buf,
    xs_buf,
    xr_buf,
    up_buf,
    res_buf,
    dlt_buf,
    ad_buf,
    ghi_buf,
    glo_buf,
    early_send,
    early_recv,
    late_send,
    late_recv,
    g_send,
    g_recv,
    h_send,
    h_recv,
    b_recv,
    acc_buf,
    in_sem,
    out_sem,
    a_send,
    a_sem,
    w_send,
    w_sem,
    p_send,
    r_sem,
    f_sem,
    x_send,
    x_sem,
    small_send,
    early_sem,
    late_sem,
    g_sem,
    h_sem,
    b_sem,
):
    dp = lax.axis_index("dp")
    t = lax.axis_index("tensor")
    z = dp // 4
    xh = (dp // 2) % 2
    c = dp % 2
    y = t // 2
    xl = t % 2
    x = 2 * xh + xl
    right = (x + 1) % NX
    left = (x + 3) % NX

    def dev(z_to, y_to, x_to, c_to):
        return (z_to * 4 + (x_to // 2) * 2 + c_to, y_to * 2 + x_to % 2)

    def remote(src, dst, send, recv, to):
        return pltpu.make_async_remote_copy(
            src_ref=src,
            dst_ref=dst,
            send_sem=send,
            recv_sem=recv,
            device_id=to,
            device_id_type=pl.DeviceIdType.MESH,
        )

    def wait_copy(ref, sem):
        pltpu.make_async_copy(ref, ref, sem).wait()

    def wait_all(ref, sems, count):
        @pl.loop(0, count)
        def _(source):
            wait_copy(ref.at[source], sems.at[source])

    to_right = dev(z, y, right, c)
    to_left = dev(z, y, left, c)
    to_core = dev(z, y, x, 1 - c)
    to_pair = dev(z, y, 2 * xh + (1 - xl), c)
    to_up = dev((z + 1) % NZ, y, x, c)
    to_down = dev((z + 7) % NZ, y, x, c)

    def a_index(x_of, c_of):
        return (x_of % 2) * 4 + (x_of // 2) * 2 + c_of

    own = a_index(x, c)
    own_a = pltpu.make_async_copy(ctx_hbm, a_buf.at[own], in_sem.at[0])
    own_a.start()
    own_w = pltpu.make_async_copy(
        w_hbm.at[:, pl.ds(pl.multiple_of(xl * 128, 128), 128)], w_buf.at[xl], w_sem.at[0]
    )
    own_w.start()
    load_up = pltpu.make_async_copy(
        up_hbm.at[:, pl.ds(pl.multiple_of(t * KB, KB), KB)], up_buf, in_sem.at[1]
    )
    load_up.start()
    load_res = pltpu.make_async_copy(res_hbm, res_buf, in_sem.at[2])
    load_res.start()
    load_dlt = pltpu.make_async_copy(dlt_hbm, dlt_buf, in_sem.at[3])
    load_dlt.start()

    barrier = pltpu.get_barrier_semaphore()

    def greet(to):
        pl.semaphore_signal(barrier, inc=1, device_id=to, device_id_type=pl.DeviceIdType.MESH)

    for step in range(1, NY):
        greet(dev(z, (y + step) % NY, x, 1 - c))
    greet(dev(z, y, 2 * (1 - xh) + (1 - xl), c))
    for step in range(1, NT):
        greet((dp, (t + step) % NT))

    @pl.loop(1, NDP)
    def _(step):
        greet(((dp + step) % NDP, t))

    pl.semaphore_wait(barrier, (NY - 1) + 1 + (NT - 1) + (NDP - 1))

    send_pair = remote(
        w_hbm.at[:, pl.ds(pl.multiple_of((1 - xl) * 128, 128), 128)],
        w_buf.at[xl],
        w_send,
        w_sem.at[1],
        to_pair,
    )
    send_pair.start()

    def send_a_rows(block, rows, sem, to):
        return remote(
            a_buf.at[block, pl.ds(rows * HALF, HALF)],
            a_buf.at[block, pl.ds(rows * HALF, HALF)],
            a_send,
            a_sem.at[sem],
            to,
        )

    def send_a_block(block, sem, to):
        return remote(a_buf.at[block], a_buf.at[block], a_send, a_sem.at[sem], to)

    def wait_a_rows(block, rows, sem):
        ref = a_buf.at[block, pl.ds(rows * HALF, HALF)]
        pltpu.make_async_copy(ref, ref, a_sem.at[sem]).wait()

    def wait_a_block(block, sem):
        ref = a_buf.at[block]
        pltpu.make_async_copy(ref, ref, a_sem.at[sem]).wait()

    own_a.wait()
    send_a_rows(own, 0, 1, to_right).start()
    send_a_rows(own, 1, 4, to_left).start()
    send_a_rows(own, 1, 2, to_right).start()
    send_a_rows(own, 0, 3, to_left).start()
    send_a_block(own, 0, to_core).start()

    def wait_w(slot, part):
        ref = w_buf.at[slot * 2 + (xl + part) % 2]
        pltpu.make_async_copy(ref, ref, w_sem.at[slot * 2 + part]).wait()

    def send_w(slot, part, to_slot, to):
        row = (xl + part) % 2
        remote(
            w_buf.at[slot * 2 + row],
            w_buf.at[to_slot * 2 + row],
            w_send,
            w_sem.at[to_slot * 2 + part],
            to,
        ).start()

    def forward(slot, part, to_slot, to):
        wait_w(slot, part)
        send_w(slot, part, to_slot, to)

    def multiply(xh_of, slots):
        total = None
        for k in range(2):
            rows = a_buf[pl.ds(k * 4 + xh_of * 2, 2)].reshape(2 * LEN, KB)
            cols = [w_buf[slot * 2 + k] for slot in slots]
            cols = cols[0] if len(cols) == 1 else jnp.concatenate(cols, axis=1)
            part = dot32(rows, cols, NN_DIMS)
            total = part if total is None else total + part
        for i, slot in enumerate(slots):
            p_buf[pl.ds(slot * 4 + xh_of * 2, 2)] = (
                total[:, i * 128 : (i + 1) * 128].astype(BF16).reshape(2, LEN, 128)
            )
        send_partials(xh_of, slots)

    offset = {0: 0, 1: 7, 2: 1, 3: 6, 4: 2, 5: 5, 6: 3, 7: 4}

    def send_partials(xh_of, slots):
        side = (xh_of + xh) % 2
        for slot in slots:
            owner = (z + offset[slot]) % NZ
            y_to = owner // 2
            group = (owner % 2) * 2 + xh_of
            away = (y_to - y + NY) % NY
            via = (y + 1 + 2 * side) % NY
            for c_of in range(2):
                src = p_buf.at[slot * 4 + xh_of * 2 + c_of]

                @pl.when((away == 0) & (c_of == c))
                def _():
                    pltpu.make_async_copy(src, r_buf.at[group, c], r_sem.at[group, c]).start()

                @pl.when((away == 0) & (c_of != c))
                def _():
                    remote(src, r_buf.at[group, c], p_send, r_sem.at[group, c], to_core).start()

                @pl.when(away == 2)
                def _():
                    index = (side * 2 + owner % 2) * 2 + c_of
                    remote(
                        src, f_buf.at[index], p_send, f_sem.at[index], dev(z, via, x, c)
                    ).start()

                @pl.when(away == 3 - 2 * side)
                def _():
                    place = 2 * (1 + away // 3) + c
                    remote(
                        src,
                        r_buf.at[group, place],
                        p_send,
                        r_sem.at[group, place],
                        dev(z, y_to, x, c_of),
                    ).start()

    def pass_sums(xh_of, slots):
        side = (xh_of + xh) % 2
        for slot in slots:
            owner = (z + offset[slot]) % NZ
            y_to = owner // 2
            group = (owner % 2) * 2 + xh_of
            away = (y_to - y + NY) % NY

            @pl.when(away == 1 + 2 * side)
            def _():
                for c_of in range(2):
                    index = (side * 2 + owner % 2) * 2 + c_of
                    wait_copy(f_buf.at[index], f_sem.at[index])
                    f_buf[index] = (
                        f_buf[index].astype(F32)
                        + p_buf[slot * 4 + xh_of * 2 + c_of].astype(F32)
                    ).astype(BF16)
                    place = 2 * (1 + away // 3) + c
                    remote(
                        f_buf.at[index],
                        r_buf.at[group, place],
                        p_send,
                        r_sem.at[group, place],
                        dev(z, y_to, x, c_of),
                    ).start()

    wait_w(0, 0)
    send_w(0, 0, 1, to_up)
    send_w(0, 0, 2, to_down)
    early_send[0:RANK] = dot32(down_ref[...], a_buf[own], NT_DIMS)
    wait_w(0, 1)
    send_w(0, 1, 1, to_up)
    send_w(0, 1, 2, to_down)
    load_up.wait()
    load_res.wait()
    load_dlt.wait()
    early_send[RANK : 2 * RANK] = dot32(up_buf[...], res_buf[...], NT_DIMS) + dot32(
        up_buf[...], dlt_buf[...], NT_DIMS
    )
    forward(1, 0, 3, to_up)
    forward(2, 0, 4, to_down)
    ones = jnp.ones((8, 128), F32)
    acc_buf[0] = jnp.zeros((LEN, 128), F32)
    for j in range(8):
        cols = pl.ds(j * 128, 128)
        target = res_buf[:, cols].astype(F32) + dlt_buf[:, cols].astype(F32)
        acc_buf[0] += target * target
    early_send[2 * RANK :] = dot_high(ones, acc_buf[0], NT_DIMS)
    for step in range(1, NT):
        remote(
            early_send, early_recv.at[t], small_send.at[0], early_sem.at[t], (dp, (t + step) % NT)
        ).start()
    pltpu.make_async_copy(early_send, early_recv.at[t], early_sem.at[t]).start()
    far = (x + 2) % NX
    wait_a_rows(a_index(left, c), 0, 1)
    send_a_rows(a_index(left, c), 0, 5, to_right).start()
    wait_a_rows(a_index(right, c), 1, 4)
    send_a_rows(a_index(right, c), 1, 6, to_left).start()
    forward(1, 1, 3, to_up)
    forward(2, 1, 4, to_down)
    wait_a_rows(a_index(left, c), 1, 2)
    send_a_block(a_index(left, c), 7, to_core).start()
    wait_a_rows(a_index(right, c), 0, 3)
    send_a_block(a_index(right, c), 8, to_core).start()
    forward(3, 0, 5, to_up)
    forward(4, 0, 6, to_down)
    wait_a_block(a_index(x, 1 - c), 0)
    wait_a_block(a_index(left, 1 - c), 7)
    wait_a_block(a_index(right, 1 - c), 8)
    multiply(xh, (0,))
    multiply(xh, (1, 2))
    forward(3, 1, 5, to_up)
    forward(4, 1, 6, to_down)
    pass_sums(xh, (0,))
    multiply(xh, (3, 4))
    pass_sums(xh, (1, 2))
    wait_a_rows(a_index(far, c), 0, 5)
    wait_a_rows(a_index(far, c), 1, 6)
    send_a_block(a_index(far, c), 9, to_core).start()
    forward(5, 0, 7, to_up)
    wait_w(6, 0)
    wait_a_block(a_index(far, 1 - c), 9)
    multiply(1 - xh, (0,))
    multiply(1 - xh, (1, 2))
    pass_sums(xh, (3, 4))
    pass_sums(1 - xh, (0,))
    multiply(1 - xh, (3, 4))
    pass_sums(1 - xh, (1, 2))
    wait_w(5, 1)
    forward(6, 1, 7, to_down)
    multiply(1 - xh, (5, 6))
    pass_sums(1 - xh, (3, 4))
    multiply(xh, (5, 6))
    wait_w(7, 0)
    wait_w(7, 1)
    multiply(1 - xh, (7,))
    multiply(xh, (7,))
    pass_sums(1 - xh, (5, 6))
    pass_sums(xh, (5, 6))
    pass_sums(1 - xh, (7,))
    pass_sums(xh, (7,))

    for xh_of in range(2):
        for xl_of in range(2):
            group = xl_of * 2 + xh_of
            x_to = xh_of * 2 + xl_of
            for source in range(6):
                wait_copy(r_buf.at[group, source], r_sem.at[group, source])
            for c_of in range(2):
                total = r_buf[group, c_of].astype(F32)
                for place in range(1, 3):
                    total = total + r_buf[group, place * 2 + c_of].astype(F32)
                xs_buf[x_to, c_of] = total.astype(BF16)

            @pl.when(x_to == x)
            def _():
                pltpu.make_async_copy(xs_buf.at[x_to], xr_buf.at[x], x_sem.at[x]).start()

            @pl.when(x_to != x)
            def _():
                remote(
                    xs_buf.at[x_to], xr_buf.at[x], x_send, x_sem.at[x], dev(z, y, x_to, c)
                ).start()

    wait_all(early_recv, early_sem, NT)
    early = early_recv[0]
    for other in range(1, NT):
        early = early + early_recv[other]
    low_rank = early[0:RANK]
    target_up = early[RANK : 2 * RANK]
    sq_target = early[2 * RANK : 2 * RANK + 1]
    low3 = split3(2.0 * low_rank)

    for source in range(NX):
        wait_copy(xr_buf.at[source], x_sem.at[source])
    for i in range(3):
        acc_buf[i] = jnp.zeros((LEN, 128), F32)
    for j in range(8):
        cols = pl.ds(j * 128, 128)
        x_of = (j // 4) * 2 + j % 2
        c_of = (j // 2) % 2
        up3 = jnp.concatenate([up_buf[:, cols]] * 3, axis=0)
        res = res_buf[:, cols].astype(F32)
        state = res + xr_buf[x_of, c_of].astype(F32) + dot32(low3, up3, TN_DIMS)
        ad_buf[:, cols] = state.astype(BF16)
        target = res + dlt_buf[:, cols].astype(F32)
        gap = state - target
        acc_buf[0] += state * state
        acc_buf[1] += state * target
        acc_buf[2] += gap * gap
        high = gap.astype(BF16)
        ghi_buf[:, cols] = high
        glo_buf[:, cols] = (gap - high.astype(F32)).astype(BF16)
    store_adapted = pltpu.make_async_copy(ad_buf, adapted_hbm, out_sem)
    store_adapted.start()
    late_send[0:RANK] = dot32(up_buf[...], ghi_buf[...], NT_DIMS) + dot32(
        up_buf[...], glo_buf[...], NT_DIMS
    )
    for i in range(3):
        late_send[RANK + 8 * i : RANK + 8 * i + 8] = dot_high(ones, acc_buf[i], NT_DIMS)
    for step in range(1, NT):
        remote(
            late_send, late_recv.at[t], small_send.at[1], late_sem.at[t], (dp, (t + step) % NT)
        ).start()
    pltpu.make_async_copy(late_send, late_recv.at[t], late_sem.at[t]).start()

    rank = lax.broadcasted_iota(jnp.int32, (1, NDP), 1)

    def total_and_here(count_ref):
        count = count_ref[...].astype(F32)
        here = jnp.where(rank == dp, count, 0.0)
        return jnp.sum(count, axis=1, keepdims=True), jnp.sum(here, axis=1, keepdims=True)

    harm_sum, harm_here = total_and_here(harm_ref)
    keep_sum, keep_here = total_and_here(keep_ref)
    position = lax.broadcasted_iota(jnp.int32, (1, LEN), 1).astype(F32)
    harmful = (position < harm_here).astype(F32)
    retained = ((position >= harm_here) & (position < harm_here + keep_here)).astype(F32)
    weight_harm = REROUTE_WEIGHT / harm_sum * harmful
    weight_keep = RETAIN_WEIGHT / keep_sum * retained

    wait_all(late_recv, late_sem, NT)
    late = late_recv[0]
    for other in range(1, NT):
        late = late + late_recv[other]
    gap_up = late[0:RANK]
    norm_h = jnp.sqrt(late[RANK : RANK + 1] + NORM_EPS)
    cross = late[RANK + 8 : RANK + 9]
    distance = jnp.sqrt(late[RANK + 16 : RANK + 17] + NORM_EPS)
    norm_g = jnp.sqrt(sq_target + NORM_EPS)
    cosine = cross / (norm_h * norm_g)
    first = weight_harm / (norm_h * norm_g)
    second = weight_harm * cosine / (norm_h * norm_h)
    third = weight_keep / distance
    by_target = 2.0 * (first - second)
    by_gap = 2.0 * (third - second)
    low_cot = by_target * target_up + by_gap * gap_up
    ga = fold3(dot32(split3(low_cot), a_buf[own], NN_DIMS))
    left_side = split3(low_rank * by_target)
    right_side = split3(low_rank * by_gap)
    gb = fold3(
        dot32(left_side, res_buf[...], NN_DIMS)
        + dot32(left_side, dlt_buf[...], NN_DIMS)
        + dot32(right_side, ghi_buf[...], NN_DIMS)
        + dot32(right_side, glo_buf[...], NN_DIMS)
    )
    for j in range(8):
        g_send[0:RANK, j, :] = ga[:, j * 128 : (j + 1) * 128]
        g_send[RANK:, j, :] = gb[:, j * 128 : (j + 1) * 128]

    @pl.loop(1, NDP)
    def _(step):
        to = (dp + step) % NDP
        remote(g_send.at[to], g_recv.at[dp], small_send.at[2], g_sem.at[dp], (to, t)).start()

    pltpu.make_async_copy(g_send.at[dp], g_recv.at[dp], g_sem.at[dp]).start()
    wait_all(g_recv, g_sem, NDP)
    total = g_recv[0]
    for other in range(1, NDP):
        total = total + g_recv[other]
    h_send[...] = total

    @pl.loop(1, NDP)
    def _(step):
        remote(
            h_send, h_recv.at[dp], small_send.at[3], h_sem.at[dp], ((dp + step) % NDP, t)
        ).start()

    pltpu.make_async_copy(h_send, h_recv.at[dp], h_sem.at[dp]).start()
    wait_all(h_recv, h_sem, NDP)
    for step in range(1, NT):
        remote(
            h_recv.at[pl.ds(RANK + 8 * c, 8)],
            b_recv.at[t, c],
            small_send.at[4],
            b_sem.at[t, 0],
            (dp, (t + step) % NT),
        ).start()
    for half in range(2):
        pltpu.make_async_copy(
            h_recv.at[pl.ds(RANK + 8 * half, 8)], b_recv.at[t, half], b_sem.at[t, half]
        ).start()
    for j in range(8):
        ga_ref[:, j * 128 : (j + 1) * 128] = h_recv[0:RANK, j, :]
    for step in range(1, NT):
        source = (t + step) % NT
        wait_copy(b_recv.at[source, c], b_sem.at[source, 0])
        remote(
            b_recv.at[source, c],
            b_recv.at[source, c],
            small_send.at[4],
            b_sem.at[source, 1],
            to_core,
        ).start()
    wait_copy(b_recv.at[t, 0], b_sem.at[t, 0])
    wait_copy(b_recv.at[t, 1], b_sem.at[t, 1])
    for step in range(1, NT):
        source = (t + step) % NT
        wait_copy(b_recv.at[source, 1 - c], b_sem.at[source, 1])
    for t_of in range(NT):
        for j in range(8):
            start = t_of * KB + j * 128
            gb_ref[0:8, start : start + 128] = b_recv[t_of, 0, :, j, :]
            gb_ref[8:16, start : start + 128] = b_recv[t_of, 1, :, j, :]

    wait_copy(a_buf.at[pl.ds(0, 7)], a_send)
    wait_copy(w_buf.at[pl.ds(0, 15)], w_send)
    wait_copy(p_buf.at[pl.ds(0, 28)], p_send)
    wait_copy(xs_buf.at[pl.ds(0, 3)], x_send)
    wait_copy(early_recv.at[pl.ds(0, NT - 1)], small_send.at[0])
    wait_copy(late_recv.at[pl.ds(0, NT - 1)], small_send.at[1])
    wait_copy(g_recv.at[pl.ds(0, NDP - 1)], small_send.at[2])
    wait_copy(h_recv.at[pl.ds(0, NDP - 1)], small_send.at[3])
    wait_copy(b_recv.at[pl.ds(0, NT - 1)], small_send.at[4])
    store_adapted.wait()


def local(ctx, w, down, up, res, dlt, harm, keep):
    vmem = pl.BlockSpec(memory_space=pltpu.VMEM)
    anyw = pl.BlockSpec(memory_space=pl.ANY)
    adapted, ga, gb = pl.pallas_call(
        kernel,
        out_shape=(
            jax.ShapeDtypeStruct((LEN, KB), BF16),
            jax.ShapeDtypeStruct((RANK, KB), F32),
            jax.ShapeDtypeStruct((RANK, NT * KB), F32),
        ),
        in_specs=[anyw, anyw, vmem, anyw, anyw, anyw, vmem, vmem],
        out_specs=(anyw, vmem, vmem),
        scratch_shapes=[
            pltpu.VMEM((8, LEN, KB), BF16),
            pltpu.VMEM((16, KB, 128), BF16),
            pltpu.VMEM((32, LEN, 128), BF16),
            pltpu.VMEM((4, 6, LEN, 128), BF16),
            pltpu.VMEM((8, LEN, 128), BF16),
            pltpu.VMEM((4, 2, LEN, 128), BF16),
            pltpu.VMEM((4, 2, LEN, 128), BF16),
            pltpu.VMEM((RANK, KB), BF16),
            pltpu.VMEM((LEN, KB), BF16),
            pltpu.VMEM((LEN, KB), BF16),
            pltpu.VMEM((LEN, KB), BF16),
            pltpu.VMEM((LEN, KB), BF16),
            pltpu.VMEM((LEN, KB), BF16),
            pltpu.VMEM((40, LEN), F32),
            pltpu.VMEM((NT, 40, LEN), F32),
            pltpu.VMEM((40, LEN), F32),
            pltpu.VMEM((NT, 40, LEN), F32),
            pltpu.VMEM((NDP, 8, 128), F32),
            pltpu.VMEM((NDP, 8, 128), F32),
            pltpu.VMEM((8, 128), F32),
            pltpu.VMEM((NDP, 8, 128), F32),
            pltpu.VMEM((NT, 2, 8, 8, 128), F32),
            pltpu.VMEM((3, LEN, 128), F32),
            pltpu.SemaphoreType.DMA((4,)),
            pltpu.SemaphoreType.DMA,
            pltpu.SemaphoreType.DMA,
            pltpu.SemaphoreType.DMA((10,)),
            pltpu.SemaphoreType.DMA,
            pltpu.SemaphoreType.DMA((16,)),
            pltpu.SemaphoreType.DMA,
            pltpu.SemaphoreType.DMA((4, 6)),
            pltpu.SemaphoreType.DMA((8,)),
            pltpu.SemaphoreType.DMA,
            pltpu.SemaphoreType.DMA((NX,)),
            pltpu.SemaphoreType.DMA((5,)),
            pltpu.SemaphoreType.DMA((NT,)),
            pltpu.SemaphoreType.DMA((NT,)),
            pltpu.SemaphoreType.DMA((NDP,)),
            pltpu.SemaphoreType.DMA((NDP,)),
            pltpu.SemaphoreType.DMA((NT, 2)),
        ],
        compiler_params=pltpu.CompilerParams(
            collective_id=0, has_side_effects=True, vmem_limit_bytes=56 * 1024 * 1024
        ),
    )(ctx, w, down.T, up, res, dlt, harm.reshape(1, NDP), keep.reshape(1, NDP))
    return adapted, ga.T, gb


def solution(mesh):
    return jax.shard_map(
        local,
        mesh=mesh,
        in_specs=(
            P("dp", "tensor"),
            P("tensor", "dp"),
            P("tensor", None),
            P(),
            P("dp", "tensor"),
            P("dp", "tensor"),
            P(),
            P(),
        ),
        out_specs=(P("dp", "tensor"), P("tensor", None), P()),
        check_vma=False,
    )
```

```python
import jax
import jax.numpy as jnp
from jax import lax
from jax.experimental import pallas as pl
from jax.experimental.pallas import tpu as pltpu
from jax.sharding import PartitionSpec as P

NORM_EPS = 1e-06
REROUTE_WEIGHT = 65536.0
RETAIN_WEIGHT = 1024.0

NZ = 8
NY = 4
NX = 4
NT = 8
NDP = 32
LEN = 384
HALF = LEN // 2
KB = 1024
RANK = 16
F32 = jnp.float32
BF16 = jnp.bfloat16
NT_DIMS = (((1,), (1,)), ((), ()))
TN_DIMS = (((0,), (0,)), ((), ()))
NN_DIMS = (((1,), (0,)), ((), ()))


def split3(value):
    hi = value.astype(BF16)
    rest = value - hi.astype(F32)
    mid = rest.astype(BF16)
    low = (rest - mid.astype(F32)).astype(BF16)
    return jnp.concatenate([hi, mid, low], axis=0)


def fold3(value):
    return value[0:RANK] + value[RANK : 2 * RANK] + value[2 * RANK : 3 * RANK]


def dot32(a, b, dims):
    return lax.dot_general(a, b, dims, preferred_element_type=F32)


def dot_high(a, b, dims):
    return lax.dot_general(a, b, dims, precision=lax.Precision.HIGHEST, preferred_element_type=F32)


def kernel(
    ctx_hbm,
    w_hbm,
    down_ref,
    up_hbm,
    res_hbm,
    dlt_hbm,
    harm_ref,
    keep_ref,
    adapted_hbm,
    ga_ref,
    gb_ref,
    a_buf,
    w_buf,
    p_buf,
    r_buf,
    f_buf,
    xs_buf,
    xr_buf,
    up_buf,
    res_buf,
    dlt_buf,
    ad_buf,
    ghi_buf,
    glo_buf,
    early_send,
    early_recv,
    late_send,
    late_recv,
    g_send,
    g_recv,
    h_send,
    h_recv,
    b_recv,
    acc_buf,
    in_sem,
    out_sem,
    a_send,
    a_sem,
    w_send,
    w_sem,
    p_send,
    r_sem,
    f_sem,
    x_send,
    x_sem,
    small_send,
    early_sem,
    late_sem,
    g_sem,
    h_sem,
    b_sem,
):
    dp = lax.axis_index("dp")
    t = lax.axis_index("tensor")
    z = dp // 4
    xh = (dp // 2) % 2
    c = dp % 2
    y = t // 2
    xl = t % 2
    x = 2 * xh + xl
    right = (x + 1) % NX
    left = (x + 3) % NX

    def dev(z_to, y_to, x_to, c_to):
        return (z_to * 4 + (x_to // 2) * 2 + c_to, y_to * 2 + x_to % 2)

    def remote(src, dst, send, recv, to):
        return pltpu.make_async_remote_copy(
            src_ref=src,
            dst_ref=dst,
            send_sem=send,
            recv_sem=recv,
            device_id=to,
            device_id_type=pl.DeviceIdType.MESH,
        )

    def wait_copy(ref, sem):
        pltpu.make_async_copy(ref, ref, sem).wait()

    def wait_all(ref, sems, count):
        @pl.loop(0, count)
        def _(source):
            wait_copy(ref.at[source], sems.at[source])

    to_right = dev(z, y, right, c)
    to_left = dev(z, y, left, c)
    to_core = dev(z, y, x, 1 - c)
    to_pair = dev(z, y, 2 * xh + (1 - xl), c)
    to_up = dev((z + 1) % NZ, y, x, c)
    to_down = dev((z + 7) % NZ, y, x, c)

    def a_index(x_of, c_of):
        return (x_of % 2) * 4 + (x_of // 2) * 2 + c_of

    own = a_index(x, c)
    own_a = pltpu.make_async_copy(ctx_hbm, a_buf.at[own], in_sem.at[0])
    own_a.start()
    own_w = pltpu.make_async_copy(
        w_hbm.at[:, pl.ds(pl.multiple_of(xl * 128, 128), 128)], w_buf.at[xl], w_sem.at[0]
    )
    own_w.start()
    load_up = pltpu.make_async_copy(
        up_hbm.at[:, pl.ds(pl.multiple_of(t * KB, KB), KB)], up_buf, in_sem.at[1]
    )
    load_up.start()
    load_res = pltpu.make_async_copy(res_hbm, res_buf, in_sem.at[2])
    load_res.start()
    load_dlt = pltpu.make_async_copy(dlt_hbm, dlt_buf, in_sem.at[3])
    load_dlt.start()

    barrier = pltpu.get_barrier_semaphore()

    def greet(to):
        pl.semaphore_signal(barrier, inc=1, device_id=to, device_id_type=pl.DeviceIdType.MESH)

    for step in range(1, NY):
        greet(dev(z, (y + step) % NY, x, 1 - c))
    for step in range(1, NT):
        greet((dp, (t + step) % NT))
    for near in (
        to_core,
        to_up,
        to_down,
        dev(z, y, 2 * (1 - xh) + (1 - xl), c),
        dev(z, y, 2 * (1 - xh) + xl, c),
        dev(z, y, 2 * (1 - xh) + xl, 1 - c),
    ):
        greet(near)
    pl.semaphore_wait(barrier, (NY - 1) + (NT - 1) + 6)

    send_pair = remote(
        w_hbm.at[:, pl.ds(pl.multiple_of((1 - xl) * 128, 128), 128)],
        w_buf.at[xl],
        w_send,
        w_sem.at[1],
        to_pair,
    )
    send_pair.start()

    def send_a_rows(block, rows, sem, to):
        return remote(
            a_buf.at[block, pl.ds(rows * HALF, HALF)],
            a_buf.at[block, pl.ds(rows * HALF, HALF)],
            a_send,
            a_sem.at[sem],
            to,
        )

    def send_a_block(block, sem, to):
        return remote(a_buf.at[block], a_buf.at[block], a_send, a_sem.at[sem], to)

    def wait_a_rows(block, rows, sem):
        ref = a_buf.at[block, pl.ds(rows * HALF, HALF)]
        pltpu.make_async_copy(ref, ref, a_sem.at[sem]).wait()

    def wait_a_block(block, sem):
        ref = a_buf.at[block]
        pltpu.make_async_copy(ref, ref, a_sem.at[sem]).wait()

    own_a.wait()
    send_a_rows(own, 0, 1, to_right).start()
    send_a_rows(own, 1, 4, to_left).start()
    send_a_rows(own, 1, 2, to_right).start()
    send_a_rows(own, 0, 3, to_left).start()
    send_a_block(own, 0, to_core).start()

    def wait_w(slot, part):
        ref = w_buf.at[slot * 2 + (xl + part) % 2]
        pltpu.make_async_copy(ref, ref, w_sem.at[slot * 2 + part]).wait()

    def send_w(slot, part, to_slot, to):
        row = (xl + part) % 2
        remote(
            w_buf.at[slot * 2 + row],
            w_buf.at[to_slot * 2 + row],
            w_send,
            w_sem.at[to_slot * 2 + part],
            to,
        ).start()

    def forward(slot, part, to_slot, to):
        wait_w(slot, part)
        send_w(slot, part, to_slot, to)

    def multiply(xh_of, slots):
        total = None
        for k in range(2):
            rows = a_buf[pl.ds(k * 4 + xh_of * 2, 2)].reshape(2 * LEN, KB)
            cols = [w_buf[slot * 2 + k] for slot in slots]
            cols = cols[0] if len(cols) == 1 else jnp.concatenate(cols, axis=1)
            part = dot32(rows, cols, NN_DIMS)
            total = part if total is None else total + part
        for i, slot in enumerate(slots):
            p_buf[pl.ds(slot * 4 + xh_of * 2, 2)] = (
                total[:, i * 128 : (i + 1) * 128].astype(BF16).reshape(2, LEN, 128)
            )
        send_partials(xh_of, slots)

    offset = {0: 0, 1: 7, 2: 1, 3: 6, 4: 2, 5: 5, 6: 3, 7: 4}

    def send_partials(xh_of, slots):
        side = (xh_of + xh) % 2
        for slot in slots:
            owner = (z + offset[slot]) % NZ
            y_to = owner // 2
            group = (owner % 2) * 2 + xh_of
            away = (y_to - y + NY) % NY
            via = (y + 1 + 2 * side) % NY
            for c_of in range(2):
                src = p_buf.at[slot * 4 + xh_of * 2 + c_of]

                @pl.when((away == 0) & (c_of == c))
                def _():
                    pltpu.make_async_copy(src, r_buf.at[group, c], r_sem.at[group, c]).start()

                @pl.when((away == 0) & (c_of != c))
                def _():
                    remote(src, r_buf.at[group, c], p_send, r_sem.at[group, c], to_core).start()

                @pl.when(away == 2)
                def _():
                    index = (side * 2 + owner % 2) * 2 + c_of
                    remote(
                        src, f_buf.at[index], p_send, f_sem.at[index], dev(z, via, x, c)
                    ).start()

                @pl.when(away == 3 - 2 * side)
                def _():
                    place = 2 * (1 + away // 3) + c
                    remote(
                        src,
                        r_buf.at[group, place],
                        p_send,
                        r_sem.at[group, place],
                        dev(z, y_to, x, c_of),
                    ).start()

    def pass_sums(xh_of, slots):
        side = (xh_of + xh) % 2
        for slot in slots:
            owner = (z + offset[slot]) % NZ
            y_to = owner // 2
            group = (owner % 2) * 2 + xh_of
            away = (y_to - y + NY) % NY

            @pl.when(away == 1 + 2 * side)
            def _():
                for c_of in range(2):
                    index = (side * 2 + owner % 2) * 2 + c_of
                    wait_copy(f_buf.at[index], f_sem.at[index])
                    f_buf[index] = (
                        f_buf[index].astype(F32)
                        + p_buf[slot * 4 + xh_of * 2 + c_of].astype(F32)
                    ).astype(BF16)
                    place = 2 * (1 + away // 3) + c
                    remote(
                        f_buf.at[index],
                        r_buf.at[group, place],
                        p_send,
                        r_sem.at[group, place],
                        dev(z, y_to, x, c_of),
                    ).start()

    wait_w(0, 0)
    send_w(0, 0, 1, to_up)
    send_w(0, 0, 2, to_down)
    early_send[0:RANK] = dot32(down_ref[...], a_buf[own], NT_DIMS)
    wait_w(0, 1)
    send_w(0, 1, 1, to_up)
    send_w(0, 1, 2, to_down)
    load_up.wait()
    load_res.wait()
    load_dlt.wait()
    early_send[RANK : 2 * RANK] = dot32(up_buf[...], res_buf[...], NT_DIMS) + dot32(
        up_buf[...], dlt_buf[...], NT_DIMS
    )
    forward(1, 0, 3, to_up)
    forward(2, 0, 4, to_down)
    ones = jnp.ones((8, 128), F32)
    acc_buf[0] = jnp.zeros((LEN, 128), F32)
    for j in range(8):
        cols = pl.ds(j * 128, 128)
        target = res_buf[:, cols].astype(F32) + dlt_buf[:, cols].astype(F32)
        acc_buf[0] += target * target
    early_send[2 * RANK :] = dot_high(ones, acc_buf[0], NT_DIMS)
    for step in range(1, NT):
        remote(
            early_send, early_recv.at[t], small_send.at[0], early_sem.at[t], (dp, (t + step) % NT)
        ).start()
    pltpu.make_async_copy(early_send, early_recv.at[t], early_sem.at[t]).start()
    far = (x + 2) % NX
    wait_a_rows(a_index(left, c), 0, 1)
    send_a_rows(a_index(left, c), 0, 5, to_right).start()
    wait_a_rows(a_index(right, c), 1, 4)
    send_a_rows(a_index(right, c), 1, 6, to_left).start()
    forward(1, 1, 3, to_up)
    forward(2, 1, 4, to_down)
    wait_a_rows(a_index(left, c), 1, 2)
    send_a_block(a_index(left, c), 7, to_core).start()
    wait_a_rows(a_index(right, c), 0, 3)
    send_a_block(a_index(right, c), 8, to_core).start()
    forward(3, 0, 5, to_up)
    forward(4, 0, 6, to_down)
    wait_a_block(a_index(x, 1 - c), 0)
    wait_a_block(a_index(left, 1 - c), 7)
    wait_a_block(a_index(right, 1 - c), 8)
    multiply(xh, (0,))
    multiply(xh, (1, 2))
    forward(3, 1, 5, to_up)
    forward(4, 1, 6, to_down)
    multiply(xh, (3, 4))
    wait_a_rows(a_index(far, c), 0, 5)
    wait_a_rows(a_index(far, c), 1, 6)
    send_a_block(a_index(far, c), 9, to_core).start()
    forward(5, 0, 7, to_up)
    wait_w(6, 0)
    wait_a_block(a_index(far, 1 - c), 9)
    multiply(1 - xh, (0,))
    pass_sums(xh, (0,))
    multiply(1 - xh, (1, 2))
    pass_sums(xh, (1, 2))
    wait_w(5, 1)
    forward(6, 1, 7, to_down)
    multiply(1 - xh, (3, 4))
    pass_sums(xh, (3, 4))
    multiply(xh, (5, 6))
    pass_sums(1 - xh, (0,))
    multiply(1 - xh, (5, 6))
    pass_sums(1 - xh, (1, 2))
    wait_w(7, 0)
    wait_w(7, 1)
    multiply(xh, (7,))
    multiply(1 - xh, (7,))
    pass_sums(1 - xh, (3, 4))
    pass_sums(xh, (5, 6))
    pass_sums(1 - xh, (5, 6))
    pass_sums(xh, (7,))
    pass_sums(1 - xh, (7,))

    for xh_of in range(2):
        for xl_of in range(2):
            group = xl_of * 2 + xh_of
            x_to = xh_of * 2 + xl_of
            for source in range(6):
                wait_copy(r_buf.at[group, source], r_sem.at[group, source])
            for c_of in range(2):
                total = r_buf[group, c_of].astype(F32)
                for place in range(1, 3):
                    total = total + r_buf[group, place * 2 + c_of].astype(F32)
                xs_buf[x_to, c_of] = total.astype(BF16)

            @pl.when(x_to == x)
            def _():
                pltpu.make_async_copy(xs_buf.at[x_to], xr_buf.at[x], x_sem.at[x]).start()

            @pl.when(x_to != x)
            def _():
                remote(
                    xs_buf.at[x_to], xr_buf.at[x], x_send, x_sem.at[x], dev(z, y, x_to, c)
                ).start()

    wait_all(early_recv, early_sem, NT)
    early = early_recv[0]
    for other in range(1, NT):
        early = early + early_recv[other]
    low_rank = early[0:RANK]
    target_up = early[RANK : 2 * RANK]
    sq_target = early[2 * RANK : 2 * RANK + 1]
    low3 = split3(2.0 * low_rank)

    for i in range(3):
        acc_buf[i] = jnp.zeros((LEN, 128), F32)
    for turn in (0, 1, 3, 2):
        x_of = (x + turn) % NX
        wait_copy(xr_buf.at[x_of], x_sem.at[x_of])
        for c_of in range(2):
            start = ((x_of // 2) * 4 + c_of * 2 + x_of % 2) * 128
            cols = pl.ds(pl.multiple_of(start, 128), 128)
            up3 = jnp.concatenate([up_buf[:, cols]] * 3, axis=0)
            res = res_buf[:, cols].astype(F32)
            state = res + xr_buf[x_of, c_of].astype(F32) + dot32(low3, up3, TN_DIMS)
            ad_buf[:, cols] = state.astype(BF16)
            target = res + dlt_buf[:, cols].astype(F32)
            gap = state - target
            acc_buf[0] += state * state
            acc_buf[1] += state * target
            acc_buf[2] += gap * gap
            high = gap.astype(BF16)
            ghi_buf[:, cols] = high
            glo_buf[:, cols] = (gap - high.astype(F32)).astype(BF16)
    store_adapted = pltpu.make_async_copy(ad_buf, adapted_hbm, out_sem)
    store_adapted.start()
    late_send[0:RANK] = dot32(up_buf[...], ghi_buf[...], NT_DIMS) + dot32(
        up_buf[...], glo_buf[...], NT_DIMS
    )
    for i in range(3):
        late_send[RANK + 8 * i : RANK + 8 * i + 8] = dot_high(ones, acc_buf[i], NT_DIMS)
    for step in range(1, NT):
        remote(
            late_send, late_recv.at[t], small_send.at[1], late_sem.at[t], (dp, (t + step) % NT)
        ).start()
    pltpu.make_async_copy(late_send, late_recv.at[t], late_sem.at[t]).start()

    rank = lax.broadcasted_iota(jnp.int32, (1, NDP), 1)

    def total_and_here(count_ref):
        count = count_ref[...].astype(F32)
        here = jnp.where(rank == dp, count, 0.0)
        return jnp.sum(count, axis=1, keepdims=True), jnp.sum(here, axis=1, keepdims=True)

    harm_sum, harm_here = total_and_here(harm_ref)
    keep_sum, keep_here = total_and_here(keep_ref)
    position = lax.broadcasted_iota(jnp.int32, (1, LEN), 1).astype(F32)
    harmful = (position < harm_here).astype(F32)
    retained = ((position >= harm_here) & (position < harm_here + keep_here)).astype(F32)
    weight_harm = REROUTE_WEIGHT / harm_sum * harmful
    weight_keep = RETAIN_WEIGHT / keep_sum * retained

    wait_all(late_recv, late_sem, NT)
    late = late_recv[0]
    for other in range(1, NT):
        late = late + late_recv[other]
    gap_up = late[0:RANK]
    norm_h = jnp.sqrt(late[RANK : RANK + 1] + NORM_EPS)
    cross = late[RANK + 8 : RANK + 9]
    distance = jnp.sqrt(late[RANK + 16 : RANK + 17] + NORM_EPS)
    norm_g = jnp.sqrt(sq_target + NORM_EPS)
    cosine = cross / (norm_h * norm_g)
    first = weight_harm / (norm_h * norm_g)
    second = weight_harm * cosine / (norm_h * norm_h)
    third = weight_keep / distance
    by_target = 2.0 * (first - second)
    by_gap = 2.0 * (third - second)
    low_cot = by_target * target_up + by_gap * gap_up
    ga = fold3(dot32(split3(low_cot), a_buf[own], NN_DIMS))
    left_side = split3(low_rank * by_target)
    right_side = split3(low_rank * by_gap)
    gb = fold3(
        dot32(left_side, res_buf[...], NN_DIMS)
        + dot32(left_side, dlt_buf[...], NN_DIMS)
        + dot32(right_side, ghi_buf[...], NN_DIMS)
        + dot32(right_side, glo_buf[...], NN_DIMS)
    )
    for j in range(8):
        g_send[0:RANK, j, :] = ga[:, j * 128 : (j + 1) * 128]
        g_send[RANK:, j, :] = gb[:, j * 128 : (j + 1) * 128]

    @pl.loop(1, NDP)
    def _(step):
        to = (dp + step) % NDP
        remote(g_send.at[to], g_recv.at[dp], small_send.at[2], g_sem.at[dp], (to, t)).start()

    pltpu.make_async_copy(g_send.at[dp], g_recv.at[dp], g_sem.at[dp]).start()
    wait_all(g_recv, g_sem, NDP)
    total = g_recv[0]
    for other in range(1, NDP):
        total = total + g_recv[other]
    h_send[...] = total

    @pl.loop(1, NDP)
    def _(step):
        remote(
            h_send, h_recv.at[dp], small_send.at[3], h_sem.at[dp], ((dp + step) % NDP, t)
        ).start()

    pltpu.make_async_copy(h_send, h_recv.at[dp], h_sem.at[dp]).start()
    wait_all(h_recv, h_sem, NDP)
    for step in range(1, NT):
        remote(
            h_recv.at[pl.ds(RANK + 8 * c, 8)],
            b_recv.at[t, c],
            small_send.at[4],
            b_sem.at[t, 0],
            (dp, (t + step) % NT),
        ).start()
    for half in range(2):
        pltpu.make_async_copy(
            h_recv.at[pl.ds(RANK + 8 * half, 8)], b_recv.at[t, half], b_sem.at[t, half]
        ).start()
    for j in range(8):
        ga_ref[:, j * 128 : (j + 1) * 128] = h_recv[0:RANK, j, :]
    for step in range(1, NT):
        source = (t + step) % NT
        wait_copy(b_recv.at[source, c], b_sem.at[source, 0])
        remote(
            b_recv.at[source, c],
            b_recv.at[source, c],
            small_send.at[4],
            b_sem.at[source, 1],
            to_core,
        ).start()
    wait_copy(b_recv.at[t, 0], b_sem.at[t, 0])
    wait_copy(b_recv.at[t, 1], b_sem.at[t, 1])
    for step in range(1, NT):
        source = (t + step) % NT
        wait_copy(b_recv.at[source, 1 - c], b_sem.at[source, 1])
    for t_of in range(NT):
        for j in range(8):
            start = t_of * KB + j * 128
            gb_ref[0:8, start : start + 128] = b_recv[t_of, 0, :, j, :]
            gb_ref[8:16, start : start + 128] = b_recv[t_of, 1, :, j, :]

    wait_copy(a_buf.at[pl.ds(0, 7)], a_send)
    wait_copy(w_buf.at[pl.ds(0, 15)], w_send)
    wait_copy(p_buf.at[pl.ds(0, 28)], p_send)
    wait_copy(xs_buf.at[pl.ds(0, 3)], x_send)
    wait_copy(early_recv.at[pl.ds(0, NT - 1)], small_send.at[0])
    wait_copy(late_recv.at[pl.ds(0, NT - 1)], small_send.at[1])
    wait_copy(g_recv.at[pl.ds(0, NDP - 1)], small_send.at[2])
    wait_copy(h_recv.at[pl.ds(0, NDP - 1)], small_send.at[3])
    wait_copy(b_recv.at[pl.ds(0, NT - 1)], small_send.at[4])
    store_adapted.wait()


def local(ctx, w, down, up, res, dlt, harm, keep):
    vmem = pl.BlockSpec(memory_space=pltpu.VMEM)
    anyw = pl.BlockSpec(memory_space=pl.ANY)
    adapted, ga, gb = pl.pallas_call(
        kernel,
        out_shape=(
            jax.ShapeDtypeStruct((LEN, KB), BF16),
            jax.ShapeDtypeStruct((RANK, KB), F32),
            jax.ShapeDtypeStruct((RANK, NT * KB), F32),
        ),
        in_specs=[anyw, anyw, vmem, anyw, anyw, anyw, vmem, vmem],
        out_specs=(anyw, vmem, vmem),
        scratch_shapes=[
            pltpu.VMEM((8, LEN, KB), BF16),
            pltpu.VMEM((16, KB, 128), BF16),
            pltpu.VMEM((32, LEN, 128), BF16),
            pltpu.VMEM((4, 6, LEN, 128), BF16),
            pltpu.VMEM((8, LEN, 128), BF16),
            pltpu.VMEM((4, 2, LEN, 128), BF16),
            pltpu.VMEM((4, 2, LEN, 128), BF16),
            pltpu.VMEM((RANK, KB), BF16),
            pltpu.VMEM((LEN, KB), BF16),
            pltpu.VMEM((LEN, KB), BF16),
            pltpu.VMEM((LEN, KB), BF16),
            pltpu.VMEM((LEN, KB), BF16),
            pltpu.VMEM((LEN, KB), BF16),
            pltpu.VMEM((40, LEN), F32),
            pltpu.VMEM((NT, 40, LEN), F32),
            pltpu.VMEM((40, LEN), F32),
            pltpu.VMEM((NT, 40, LEN), F32),
            pltpu.VMEM((NDP, 8, 128), F32),
            pltpu.VMEM((NDP, 8, 128), F32),
            pltpu.VMEM((8, 128), F32),
            pltpu.VMEM((NDP, 8, 128), F32),
            pltpu.VMEM((NT, 2, 8, 8, 128), F32),
            pltpu.VMEM((3, LEN, 128), F32),
            pltpu.SemaphoreType.DMA((4,)),
            pltpu.SemaphoreType.DMA,
            pltpu.SemaphoreType.DMA,
            pltpu.SemaphoreType.DMA((10,)),
            pltpu.SemaphoreType.DMA,
            pltpu.SemaphoreType.DMA((16,)),
            pltpu.SemaphoreType.DMA,
            pltpu.SemaphoreType.DMA((4, 6)),
            pltpu.SemaphoreType.DMA((8,)),
            pltpu.SemaphoreType.DMA,
            pltpu.SemaphoreType.DMA((NX,)),
            pltpu.SemaphoreType.DMA((5,)),
            pltpu.SemaphoreType.DMA((NT,)),
            pltpu.SemaphoreType.DMA((NT,)),
            pltpu.SemaphoreType.DMA((NDP,)),
            pltpu.SemaphoreType.DMA((NDP,)),
            pltpu.SemaphoreType.DMA((NT, 2)),
        ],
        compiler_params=pltpu.CompilerParams(
            collective_id=0, has_side_effects=True, vmem_limit_bytes=56 * 1024 * 1024
        ),
    )(ctx, w, down.T, up, res, dlt, harm.reshape(1, NDP), keep.reshape(1, NDP))
    return adapted, ga.T, gb


def solution(mesh):
    return jax.shard_map(
        local,
        mesh=mesh,
        in_specs=(
            P("dp", "tensor"),
            P("tensor", "dp"),
            P("tensor", None),
            P(),
            P("dp", "tensor"),
            P("dp", "tensor"),
            P(),
            P(),
        ),
        out_specs=(P("dp", "tensor"), P("tensor", None), P()),
        check_vma=False,
    )
```

```python
import jax
import jax.numpy as jnp
from jax import lax
from jax.experimental import pallas as pl
from jax.experimental.pallas import tpu as pltpu
from jax.sharding import PartitionSpec as P

NORM_EPS = 1e-06
REROUTE_WEIGHT = 65536.0
RETAIN_WEIGHT = 1024.0

NZ = 8
NY = 4
NX = 4
NT = 8
NDP = 32
LEN = 384
HALF = LEN // 2
KB = 1024
RANK = 16
F32 = jnp.float32
BF16 = jnp.bfloat16
NT_DIMS = (((1,), (1,)), ((), ()))
TN_DIMS = (((0,), (0,)), ((), ()))
NN_DIMS = (((1,), (0,)), ((), ()))


def split3(value):
    hi = value.astype(BF16)
    rest = value - hi.astype(F32)
    mid = rest.astype(BF16)
    low = (rest - mid.astype(F32)).astype(BF16)
    return jnp.concatenate([hi, mid, low], axis=0)


def fold3(value):
    return value[0:RANK] + value[RANK : 2 * RANK] + value[2 * RANK : 3 * RANK]


def dot32(a, b, dims):
    return lax.dot_general(a, b, dims, preferred_element_type=F32)


def dot_high(a, b, dims):
    return lax.dot_general(a, b, dims, precision=lax.Precision.HIGHEST, preferred_element_type=F32)


def kernel(
    ctx_hbm,
    w_hbm,
    down_ref,
    up_hbm,
    res_hbm,
    dlt_hbm,
    harm_ref,
    keep_ref,
    adapted_hbm,
    ga_ref,
    gb_ref,
    a_buf,
    w_buf,
    p_buf,
    r_buf,
    f_buf,
    xs_buf,
    xr_buf,
    up_buf,
    res_buf,
    dlt_buf,
    ad_buf,
    ghi_buf,
    glo_buf,
    early_send,
    early_recv,
    late_send,
    late_recv,
    g_send,
    g_recv,
    h_send,
    h_recv,
    b_recv,
    acc_buf,
    in_sem,
    out_sem,
    a_send,
    a_sem,
    w_send,
    w_sem,
    p_send,
    r_sem,
    f_sem,
    x_send,
    x_sem,
    small_send,
    early_sem,
    late_sem,
    g_sem,
    h_sem,
    b_sem,
):
    dp = lax.axis_index("dp")
    t = lax.axis_index("tensor")
    z = dp // 4
    xh = (dp // 2) % 2
    c = dp % 2
    y = t // 2
    xl = t % 2
    x = 2 * xh + xl
    right = (x + 1) % NX
    left = (x + 3) % NX

    def dev(z_to, y_to, x_to, c_to):
        return (z_to * 4 + (x_to // 2) * 2 + c_to, y_to * 2 + x_to % 2)

    def remote(src, dst, send, recv, to):
        return pltpu.make_async_remote_copy(
            src_ref=src,
            dst_ref=dst,
            send_sem=send,
            recv_sem=recv,
            device_id=to,
            device_id_type=pl.DeviceIdType.MESH,
        )

    def wait_copy(ref, sem):
        pltpu.make_async_copy(ref, ref, sem).wait()

    def wait_all(ref, sems, count):
        @pl.loop(0, count)
        def _(source):
            wait_copy(ref.at[source], sems.at[source])

    to_right = dev(z, y, right, c)
    to_left = dev(z, y, left, c)
    to_core = dev(z, y, x, 1 - c)
    to_pair = dev(z, y, 2 * xh + (1 - xl), c)
    to_up = dev((z + 1) % NZ, y, x, c)
    to_down = dev((z + 7) % NZ, y, x, c)

    def a_index(x_of, c_of):
        return (x_of % 2) * 4 + (x_of // 2) * 2 + c_of

    own = a_index(x, c)
    own_a = pltpu.make_async_copy(ctx_hbm, a_buf.at[own], in_sem.at[0])
    own_a.start()
    own_w = pltpu.make_async_copy(
        w_hbm.at[:, pl.ds(pl.multiple_of(xl * 128, 128), 128)], w_buf.at[xl], w_sem.at[0]
    )
    own_w.start()
    load_up = pltpu.make_async_copy(
        up_hbm.at[:, pl.ds(pl.multiple_of(t * KB, KB), KB)], up_buf, in_sem.at[1]
    )
    load_up.start()
    load_res = pltpu.make_async_copy(res_hbm, res_buf, in_sem.at[2])
    load_res.start()
    load_dlt = pltpu.make_async_copy(dlt_hbm, dlt_buf, in_sem.at[3])
    load_dlt.start()

    barrier = pltpu.get_barrier_semaphore()

    def greet(to):
        pl.semaphore_signal(barrier, inc=1, device_id=to, device_id_type=pl.DeviceIdType.MESH)

    for step in range(1, NY):
        greet(dev(z, (y + step) % NY, x, 1 - c))
    for step in range(1, NT):
        greet((dp, (t + step) % NT))
    for near in (
        to_core,
        to_up,
        to_down,
        dev(z, y, 2 * (1 - xh) + (1 - xl), c),
        dev(z, y, 2 * (1 - xh) + xl, c),
        dev(z, y, 2 * (1 - xh) + xl, 1 - c),
    ):
        greet(near)
    pl.semaphore_wait(barrier, (NY - 1) + (NT - 1) + 6)

    send_pair = remote(
        w_hbm.at[:, pl.ds(pl.multiple_of((1 - xl) * 128, 128), 128)],
        w_buf.at[xl],
        w_send,
        w_sem.at[1],
        to_pair,
    )
    send_pair.start()

    def send_a_rows(block, rows, sem, to):
        return remote(
            a_buf.at[block, pl.ds(rows * HALF, HALF)],
            a_buf.at[block, pl.ds(rows * HALF, HALF)],
            a_send,
            a_sem.at[sem],
            to,
        )

    def send_a_block(block, sem, to):
        return remote(a_buf.at[block], a_buf.at[block], a_send, a_sem.at[sem], to)

    def wait_a_rows(block, rows, sem):
        ref = a_buf.at[block, pl.ds(rows * HALF, HALF)]
        pltpu.make_async_copy(ref, ref, a_sem.at[sem]).wait()

    def wait_a_block(block, sem):
        ref = a_buf.at[block]
        pltpu.make_async_copy(ref, ref, a_sem.at[sem]).wait()

    own_a.wait()
    send_a_rows(own, 0, 1, to_right).start()
    send_a_rows(own, 1, 4, to_left).start()
    send_a_rows(own, 1, 2, to_right).start()
    send_a_rows(own, 0, 3, to_left).start()
    send_a_block(own, 0, to_core).start()

    def wait_w(slot, part):
        ref = w_buf.at[slot * 2 + (xl + part) % 2]
        pltpu.make_async_copy(ref, ref, w_sem.at[slot * 2 + part]).wait()

    def send_w(slot, part, to_slot, to):
        row = (xl + part) % 2
        remote(
            w_buf.at[slot * 2 + row],
            w_buf.at[to_slot * 2 + row],
            w_send,
            w_sem.at[to_slot * 2 + part],
            to,
        ).start()

    def forward(slot, part, to_slot, to):
        wait_w(slot, part)
        send_w(slot, part, to_slot, to)

    def multiply(xh_of, slots):
        total = None
        for k in range(2):
            rows = a_buf[pl.ds(k * 4 + xh_of * 2, 2)].reshape(2 * LEN, KB)
            cols = [w_buf[slot * 2 + k] for slot in slots]
            cols = cols[0] if len(cols) == 1 else jnp.concatenate(cols, axis=1)
            part = dot32(rows, cols, NN_DIMS)
            total = part if total is None else total + part
        for i, slot in enumerate(slots):
            p_buf[pl.ds(slot * 4 + xh_of * 2, 2)] = (
                total[:, i * 128 : (i + 1) * 128].astype(BF16).reshape(2, LEN, 128)
            )
        send_partials(xh_of, slots)

    offset = {0: 0, 1: 7, 2: 1, 3: 6, 4: 2, 5: 5, 6: 3, 7: 4}

    def route(xh_of, slot):
        side = (xh_of + xh) % 2
        owner = (z + offset[slot]) % NZ
        group = (owner % 2) * 2 + xh_of
        away = ((owner // 2 - y + NY) * (1 + 2 * side)) % NY
        onward = (y + 1 + 2 * side) % NY

        def place(stage, c_of):
            return ((side * 2 + stage) * 2 + owner % 2) * 2 + c_of

        return group, away, onward, place

    def send_partials(xh_of, slots):
        for slot in slots:
            group, away, onward, place = route(xh_of, slot)
            for c_of in range(2):
                src = p_buf.at[slot * 4 + xh_of * 2 + c_of]
                start = place(0, c_of)

                @pl.when((away == 0) & (c_of == c))
                def _():
                    pltpu.make_async_copy(src, r_buf.at[group, c], r_sem.at[group, c]).start()

                @pl.when((away == 0) & (c_of != c))
                def _():
                    remote(src, r_buf.at[group, c], p_send, r_sem.at[group, c], to_core).start()

                @pl.when(away == 3)
                def _():
                    remote(
                        src, f_buf.at[start], p_send, f_sem.at[start], dev(z, onward, x, c)
                    ).start()

    def pass_sums(xh_of, slots):
        for slot in slots:
            group, away, onward, place = route(xh_of, slot)

            def add(index, c_of):
                wait_copy(f_buf.at[index], f_sem.at[index])
                f_buf[index] = (
                    f_buf[index].astype(F32) + p_buf[slot * 4 + xh_of * 2 + c_of].astype(F32)
                ).astype(BF16)

            @pl.when(away == 2)
            def _():
                for c_of in range(2):
                    index = place(0, c_of)
                    after = place(1, c_of)
                    add(index, c_of)
                    remote(
                        f_buf.at[index], f_buf.at[after], p_send, f_sem.at[after], dev(z, onward, x, c)
                    ).start()

            @pl.when(away == 1)
            def _():
                for c_of in range(2):
                    index = place(1, c_of)
                    add(index, c_of)
                    remote(
                        f_buf.at[index],
                        r_buf.at[group, 2 + c],
                        p_send,
                        r_sem.at[group, 2 + c],
                        dev(z, onward, x, c_of),
                    ).start()

    wait_w(0, 0)
    send_w(0, 0, 1, to_up)
    send_w(0, 0, 2, to_down)
    early_send[0:RANK] = dot32(down_ref[...], a_buf[own], NT_DIMS)
    wait_w(0, 1)
    send_w(0, 1, 1, to_up)
    send_w(0, 1, 2, to_down)
    load_up.wait()
    load_res.wait()
    load_dlt.wait()
    early_send[RANK : 2 * RANK] = dot32(up_buf[...], res_buf[...], NT_DIMS) + dot32(
        up_buf[...], dlt_buf[...], NT_DIMS
    )
    forward(1, 0, 3, to_up)
    forward(2, 0, 4, to_down)
    ones = jnp.ones((8, 128), F32)
    acc_buf[0] = jnp.zeros((LEN, 128), F32)
    for j in range(8):
        cols = pl.ds(j * 128, 128)
        target = res_buf[:, cols].astype(F32) + dlt_buf[:, cols].astype(F32)
        acc_buf[0] += target * target
    early_send[2 * RANK :] = dot_high(ones, acc_buf[0], NT_DIMS)
    for step in range(1, NT):
        remote(
            early_send, early_recv.at[t], small_send.at[0], early_sem.at[t], (dp, (t + step) % NT)
        ).start()
    pltpu.make_async_copy(early_send, early_recv.at[t], early_sem.at[t]).start()
    far = (x + 2) % NX
    wait_a_rows(a_index(left, c), 0, 1)
    send_a_rows(a_index(left, c), 0, 5, to_right).start()
    wait_a_rows(a_index(right, c), 1, 4)
    send_a_rows(a_index(right, c), 1, 6, to_left).start()
    forward(1, 1, 3, to_up)
    forward(2, 1, 4, to_down)
    wait_a_rows(a_index(left, c), 1, 2)
    send_a_block(a_index(left, c), 7, to_core).start()
    wait_a_rows(a_index(right, c), 0, 3)
    send_a_block(a_index(right, c), 8, to_core).start()
    forward(3, 0, 5, to_up)
    forward(4, 0, 6, to_down)
    wait_a_block(a_index(x, 1 - c), 0)
    wait_a_block(a_index(left, 1 - c), 7)
    wait_a_block(a_index(right, 1 - c), 8)
    multiply(xh, (0,))
    multiply(xh, (1, 2))
    forward(3, 1, 5, to_up)
    forward(4, 1, 6, to_down)
    multiply(xh, (3, 4))
    wait_a_rows(a_index(far, c), 0, 5)
    wait_a_rows(a_index(far, c), 1, 6)
    send_a_block(a_index(far, c), 9, to_core).start()
    forward(5, 0, 7, to_up)
    wait_w(6, 0)
    wait_a_block(a_index(far, 1 - c), 9)
    multiply(1 - xh, (0,))
    pass_sums(xh, (0,))
    multiply(1 - xh, (1, 2))
    pass_sums(xh, (1, 2))
    wait_w(5, 1)
    forward(6, 1, 7, to_down)
    multiply(1 - xh, (3, 4))
    pass_sums(xh, (3, 4))
    multiply(xh, (5, 6))
    pass_sums(1 - xh, (0,))
    multiply(1 - xh, (5, 6))
    pass_sums(1 - xh, (1, 2))
    wait_w(7, 0)
    wait_w(7, 1)
    multiply(1 - xh, (7,))
    multiply(xh, (7,))
    pass_sums(1 - xh, (3, 4))
    pass_sums(1 - xh, (5, 6))
    pass_sums(xh, (5, 6))
    pass_sums(1 - xh, (7,))
    pass_sums(xh, (7,))

    for turn in (2, 1, 3, 0):
        x_to = (x + turn) % NX
        group = (x_to % 2) * 2 + x_to // 2
        for source in range(4):
            wait_copy(r_buf.at[group, source], r_sem.at[group, source])
        for c_of in range(2):
            total = r_buf[group, c_of].astype(F32) + r_buf[group, 2 + c_of].astype(F32)
            xs_buf[x_to, c_of] = total.astype(BF16)
        if turn == 0:
            pltpu.make_async_copy(xs_buf.at[x_to], xr_buf.at[x], x_sem.at[x]).start()
        else:
            remote(
                xs_buf.at[x_to], xr_buf.at[x], x_send, x_sem.at[x], dev(z, y, x_to, c)
            ).start()

    wait_all(early_recv, early_sem, NT)
    early = early_recv[0]
    for other in range(1, NT):
        early = early + early_recv[other]
    low_rank = early[0:RANK]
    target_up = early[RANK : 2 * RANK]
    sq_target = early[2 * RANK : 2 * RANK + 1]
    low3 = split3(2.0 * low_rank)

    for i in range(3):
        acc_buf[i] = jnp.zeros((LEN, 128), F32)
    for turn in (0, 1, 3, 2):
        x_of = (x + turn) % NX
        wait_copy(xr_buf.at[x_of], x_sem.at[x_of])
        for c_of in range(2):
            start = ((x_of // 2) * 4 + c_of * 2 + x_of % 2) * 128
            cols = pl.ds(pl.multiple_of(start, 128), 128)
            up3 = jnp.concatenate([up_buf[:, cols]] * 3, axis=0)
            res = res_buf[:, cols].astype(F32)
            state = res + xr_buf[x_of, c_of].astype(F32) + dot32(low3, up3, TN_DIMS)
            ad_buf[:, cols] = state.astype(BF16)
            target = res + dlt_buf[:, cols].astype(F32)
            gap = state - target
            acc_buf[0] += state * state
            acc_buf[1] += state * target
            acc_buf[2] += gap * gap
            high = gap.astype(BF16)
            ghi_buf[:, cols] = high
            glo_buf[:, cols] = (gap - high.astype(F32)).astype(BF16)
    store_adapted = pltpu.make_async_copy(ad_buf, adapted_hbm, out_sem)
    store_adapted.start()
    late_send[0:RANK] = dot32(up_buf[...], ghi_buf[...], NT_DIMS) + dot32(
        up_buf[...], glo_buf[...], NT_DIMS
    )
    row = lax.broadcasted_iota(jnp.int32, (8, 128), 0)
    stats = None
    for i in range(3):
        part = dot_high((row == i).astype(F32), acc_buf[i], NT_DIMS)
        stats = part if stats is None else stats + part
    late_send[RANK:] = stats
    for step in range(1, NT):
        remote(
            late_send, late_recv.at[t], small_send.at[1], late_sem.at[t], (dp, (t + step) % NT)
        ).start()
    pltpu.make_async_copy(late_send, late_recv.at[t], late_sem.at[t]).start()

    rank = lax.broadcasted_iota(jnp.int32, (1, NDP), 1)

    def total_and_here(count_ref):
        count = count_ref[...].astype(F32)
        here = jnp.where(rank == dp, count, 0.0)
        return jnp.sum(count, axis=1, keepdims=True), jnp.sum(here, axis=1, keepdims=True)

    harm_sum, harm_here = total_and_here(harm_ref)
    keep_sum, keep_here = total_and_here(keep_ref)
    position = lax.broadcasted_iota(jnp.int32, (1, LEN), 1).astype(F32)
    harmful = (position < harm_here).astype(F32)
    retained = ((position >= harm_here) & (position < harm_here + keep_here)).astype(F32)
    weight_harm = REROUTE_WEIGHT / harm_sum * harmful
    weight_keep = RETAIN_WEIGHT / keep_sum * retained

    wait_all(late_recv, late_sem, NT)
    late = late_recv[0]
    for other in range(1, NT):
        late = late + late_recv[other]
    gap_up = late[0:RANK]
    norm_h = jnp.sqrt(late[RANK : RANK + 1] + NORM_EPS)
    cross = late[RANK + 1 : RANK + 2]
    distance = jnp.sqrt(late[RANK + 2 : RANK + 3] + NORM_EPS)
    norm_g = jnp.sqrt(sq_target + NORM_EPS)
    cosine = cross / (norm_h * norm_g)
    first = weight_harm / (norm_h * norm_g)
    second = weight_harm * cosine / (norm_h * norm_h)
    third = weight_keep / distance
    by_target = 2.0 * (first - second)
    by_gap = 2.0 * (third - second)
    low_cot = by_target * target_up + by_gap * gap_up
    ga = fold3(dot32(split3(low_cot), a_buf[own], NN_DIMS))
    left_side = split3(low_rank * by_target)
    right_side = split3(low_rank * by_gap)
    gb = fold3(
        dot32(left_side, res_buf[...], NN_DIMS)
        + dot32(left_side, dlt_buf[...], NN_DIMS)
        + dot32(right_side, ghi_buf[...], NN_DIMS)
        + dot32(right_side, glo_buf[...], NN_DIMS)
    )
    for j in range(8):
        g_send[0:RANK, j, :] = ga[:, j * 128 : (j + 1) * 128]
        g_send[RANK:, j, :] = gb[:, j * 128 : (j + 1) * 128]

    @pl.loop(1, NDP)
    def _(step):
        to = (dp + step) % NDP
        remote(g_send.at[to], g_recv.at[dp], small_send.at[2], g_sem.at[dp], (to, t)).start()

    pltpu.make_async_copy(g_send.at[dp], g_recv.at[dp], g_sem.at[dp]).start()
    wait_all(g_recv, g_sem, NDP)
    total = g_recv[0]
    for other in range(1, NDP):
        total = total + g_recv[other]
    h_send[...] = total

    @pl.loop(1, NDP)
    def _(step):
        remote(
            h_send, h_recv.at[dp], small_send.at[3], h_sem.at[dp], ((dp + step) % NDP, t)
        ).start()

    pltpu.make_async_copy(h_send, h_recv.at[dp], h_sem.at[dp]).start()
    wait_all(h_recv, h_sem, NDP)
    for step in range(1, NT):
        remote(
            h_recv.at[pl.ds(RANK + 8 * c, 8)],
            b_recv.at[t, c],
            small_send.at[4],
            b_sem.at[t, 0],
            (dp, (t + step) % NT),
        ).start()
    for half in range(2):
        pltpu.make_async_copy(
            h_recv.at[pl.ds(RANK + 8 * half, 8)], b_recv.at[t, half], b_sem.at[t, half]
        ).start()
    for j in range(8):
        ga_ref[:, j * 128 : (j + 1) * 128] = h_recv[0:RANK, j, :]
    for step in range(1, NT):
        source = (t + step) % NT
        wait_copy(b_recv.at[source, c], b_sem.at[source, 0])
        remote(
            b_recv.at[source, c],
            b_recv.at[source, c],
            small_send.at[4],
            b_sem.at[source, 1],
            to_core,
        ).start()
    wait_copy(b_recv.at[t, 0], b_sem.at[t, 0])
    wait_copy(b_recv.at[t, 1], b_sem.at[t, 1])
    for step in range(1, NT):
        source = (t + step) % NT
        wait_copy(b_recv.at[source, 1 - c], b_sem.at[source, 1])
    for t_of in range(NT):
        for j in range(8):
            start = t_of * KB + j * 128
            gb_ref[0:8, start : start + 128] = b_recv[t_of, 0, :, j, :]
            gb_ref[8:16, start : start + 128] = b_recv[t_of, 1, :, j, :]

    wait_copy(a_buf.at[pl.ds(0, 7)], a_send)
    wait_copy(w_buf.at[pl.ds(0, 15)], w_send)
    wait_copy(p_buf.at[pl.ds(0, 28)], p_send)
    wait_copy(xs_buf.at[pl.ds(0, 3)], x_send)
    wait_copy(early_recv.at[pl.ds(0, NT - 1)], small_send.at[0])
    wait_copy(late_recv.at[pl.ds(0, NT - 1)], small_send.at[1])
    wait_copy(g_recv.at[pl.ds(0, NDP - 1)], small_send.at[2])
    wait_copy(h_recv.at[pl.ds(0, NDP - 1)], small_send.at[3])
    wait_copy(b_recv.at[pl.ds(0, NT - 1)], small_send.at[4])
    store_adapted.wait()


def local(ctx, w, down, up, res, dlt, harm, keep):
    vmem = pl.BlockSpec(memory_space=pltpu.VMEM)
    anyw = pl.BlockSpec(memory_space=pl.ANY)
    adapted, ga, gb = pl.pallas_call(
        kernel,
        out_shape=(
            jax.ShapeDtypeStruct((LEN, KB), BF16),
            jax.ShapeDtypeStruct((RANK, KB), F32),
            jax.ShapeDtypeStruct((RANK, NT * KB), F32),
        ),
        in_specs=[anyw, anyw, vmem, anyw, anyw, anyw, vmem, vmem],
        out_specs=(anyw, vmem, vmem),
        scratch_shapes=[
            pltpu.VMEM((8, LEN, KB), BF16),
            pltpu.VMEM((16, KB, 128), BF16),
            pltpu.VMEM((32, LEN, 128), BF16),
            pltpu.VMEM((4, 4, LEN, 128), BF16),
            pltpu.VMEM((16, LEN, 128), BF16),
            pltpu.VMEM((4, 2, LEN, 128), BF16),
            pltpu.VMEM((4, 2, LEN, 128), BF16),
            pltpu.VMEM((RANK, KB), BF16),
            pltpu.VMEM((LEN, KB), BF16),
            pltpu.VMEM((LEN, KB), BF16),
            pltpu.VMEM((LEN, KB), BF16),
            pltpu.VMEM((LEN, KB), BF16),
            pltpu.VMEM((LEN, KB), BF16),
            pltpu.VMEM((40, LEN), F32),
            pltpu.VMEM((NT, 40, LEN), F32),
            pltpu.VMEM((24, LEN), F32),
            pltpu.VMEM((NT, 24, LEN), F32),
            pltpu.VMEM((NDP, 8, 128), F32),
            pltpu.VMEM((NDP, 8, 128), F32),
            pltpu.VMEM((8, 128), F32),
            pltpu.VMEM((NDP, 8, 128), F32),
            pltpu.VMEM((NT, 2, 8, 8, 128), F32),
            pltpu.VMEM((3, LEN, 128), F32),
            pltpu.SemaphoreType.DMA((4,)),
            pltpu.SemaphoreType.DMA,
            pltpu.SemaphoreType.DMA,
            pltpu.SemaphoreType.DMA((10,)),
            pltpu.SemaphoreType.DMA,
            pltpu.SemaphoreType.DMA((16,)),
            pltpu.SemaphoreType.DMA,
            pltpu.SemaphoreType.DMA((4, 4)),
            pltpu.SemaphoreType.DMA((16,)),
            pltpu.SemaphoreType.DMA,
            pltpu.SemaphoreType.DMA((NX,)),
            pltpu.SemaphoreType.DMA((5,)),
            pltpu.SemaphoreType.DMA((NT,)),
            pltpu.SemaphoreType.DMA((NT,)),
            pltpu.SemaphoreType.DMA((NDP,)),
            pltpu.SemaphoreType.DMA((NDP,)),
            pltpu.SemaphoreType.DMA((NT, 2)),
        ],
        compiler_params=pltpu.CompilerParams(
            collective_id=0, has_side_effects=True, vmem_limit_bytes=56 * 1024 * 1024
        ),
    )(ctx, w, down.T, up, res, dlt, harm.reshape(1, NDP), keep.reshape(1, NDP))
    return adapted, ga.T, gb


def solution(mesh):
    return jax.shard_map(
        local,
        mesh=mesh,
        in_specs=(
            P("dp", "tensor"),
            P("tensor", "dp"),
            P("tensor", None),
            P(),
            P("dp", "tensor"),
            P("dp", "tensor"),
            P(),
            P(),
        ),
        out_specs=(P("dp", "tensor"), P("tensor", None), P()),
        check_vma=False,
    )
```

```python
import jax
import jax.numpy as jnp
from jax import lax
from jax.experimental import pallas as pl
from jax.experimental.pallas import tpu as pltpu
from jax.sharding import PartitionSpec as P

NORM_EPS = 1e-06
REROUTE_WEIGHT = 65536.0
RETAIN_WEIGHT = 1024.0

NZ = 8
NY = 4
NX = 4
NT = 8
NDP = 32
LEN = 384
HALF = LEN // 2
KB = 1024
RANK = 16
F32 = jnp.float32
BF16 = jnp.bfloat16
NT_DIMS = (((1,), (1,)), ((), ()))
TN_DIMS = (((0,), (0,)), ((), ()))
NN_DIMS = (((1,), (0,)), ((), ()))


def split3(value):
    hi = value.astype(BF16)
    rest = value - hi.astype(F32)
    mid = rest.astype(BF16)
    low = (rest - mid.astype(F32)).astype(BF16)
    return jnp.concatenate([hi, mid, low], axis=0)


def fold3(value):
    return value[0:RANK] + value[RANK : 2 * RANK] + value[2 * RANK : 3 * RANK]


def dot32(a, b, dims):
    return lax.dot_general(a, b, dims, preferred_element_type=F32)


def dot_high(a, b, dims):
    return lax.dot_general(a, b, dims, precision=lax.Precision.HIGHEST, preferred_element_type=F32)


def kernel(
    ctx_hbm,
    w_hbm,
    down_ref,
    up_hbm,
    res_hbm,
    dlt_hbm,
    harm_ref,
    keep_ref,
    adapted_hbm,
    ga_ref,
    gb_ref,
    a_buf,
    w_buf,
    p_buf,
    r_buf,
    f_buf,
    xs_buf,
    xr_buf,
    up_buf,
    res_buf,
    dlt_buf,
    ad_buf,
    ghi_buf,
    glo_buf,
    early_send,
    early_recv,
    late_send,
    late_recv,
    g_send,
    g_recv,
    h_send,
    h_recv,
    b_recv,
    acc_buf,
    in_sem,
    out_sem,
    a_send,
    a_sem,
    w_send,
    w_sem,
    p_send,
    r_sem,
    f_sem,
    x_send,
    x_sem,
    small_send,
    early_sem,
    late_sem,
    g_sem,
    h_sem,
    b_sem,
):
    dp = lax.axis_index("dp")
    t = lax.axis_index("tensor")
    z = dp // 4
    xh = (dp // 2) % 2
    c = dp % 2
    y = t // 2
    xl = t % 2
    x = 2 * xh + xl
    right = (x + 1) % NX
    left = (x + 3) % NX

    def dev(z_to, y_to, x_to, c_to):
        return (z_to * 4 + (x_to // 2) * 2 + c_to, y_to * 2 + x_to % 2)

    def remote(src, dst, send, recv, to):
        return pltpu.make_async_remote_copy(
            src_ref=src,
            dst_ref=dst,
            send_sem=send,
            recv_sem=recv,
            device_id=to,
            device_id_type=pl.DeviceIdType.MESH,
        )

    def wait_copy(ref, sem):
        pltpu.make_async_copy(ref, ref, sem).wait()

    def wait_all(ref, sems, count):
        @pl.loop(0, count)
        def _(source):
            wait_copy(ref.at[source], sems.at[source])

    to_right = dev(z, y, right, c)
    to_left = dev(z, y, left, c)
    to_core = dev(z, y, x, 1 - c)
    to_pair = dev(z, y, 2 * xh + (1 - xl), c)
    to_up = dev((z + 1) % NZ, y, x, c)
    to_down = dev((z + 7) % NZ, y, x, c)

    def a_index(x_of, c_of):
        return (x_of % 2) * 4 + (x_of // 2) * 2 + c_of

    own = a_index(x, c)
    own_a = pltpu.make_async_copy(ctx_hbm, a_buf.at[own], in_sem.at[0])
    own_a.start()
    own_w = pltpu.make_async_copy(
        w_hbm.at[:, pl.ds(pl.multiple_of(xl * 128, 128), 128)], w_buf.at[xl], w_sem.at[0]
    )
    own_w.start()
    load_up = pltpu.make_async_copy(
        up_hbm.at[:, pl.ds(pl.multiple_of(t * KB, KB), KB)], up_buf, in_sem.at[1]
    )
    load_up.start()
    load_res = pltpu.make_async_copy(res_hbm, res_buf, in_sem.at[2])
    load_res.start()
    load_dlt = pltpu.make_async_copy(dlt_hbm, dlt_buf, in_sem.at[3])
    load_dlt.start()

    barrier = pltpu.get_barrier_semaphore()

    def greet(to):
        pl.semaphore_signal(barrier, inc=1, device_id=to, device_id_type=pl.DeviceIdType.MESH)

    for step in range(1, NY):
        greet(dev(z, (y + step) % NY, x, 1 - c))
    for step in range(1, NT):
        greet((dp, (t + step) % NT))
    for near in (
        to_core,
        to_up,
        to_down,
        dev(z, y, 2 * (1 - xh) + (1 - xl), c),
        dev(z, y, 2 * (1 - xh) + xl, c),
        dev(z, y, 2 * (1 - xh) + xl, 1 - c),
    ):
        greet(near)
    pl.semaphore_wait(barrier, (NY - 1) + (NT - 1) + 6)

    send_pair = remote(
        w_hbm.at[:, pl.ds(pl.multiple_of((1 - xl) * 128, 128), 128)],
        w_buf.at[xl],
        w_send,
        w_sem.at[1],
        to_pair,
    )
    send_pair.start()

    def send_a_rows(block, rows, sem, to):
        return remote(
            a_buf.at[block, pl.ds(rows * HALF, HALF)],
            a_buf.at[block, pl.ds(rows * HALF, HALF)],
            a_send,
            a_sem.at[sem],
            to,
        )

    def send_a_block(block, sem, to):
        return remote(a_buf.at[block], a_buf.at[block], a_send, a_sem.at[sem], to)

    def wait_a_rows(block, rows, sem):
        ref = a_buf.at[block, pl.ds(rows * HALF, HALF)]
        pltpu.make_async_copy(ref, ref, a_sem.at[sem]).wait()

    def wait_a_block(block, sem):
        ref = a_buf.at[block]
        pltpu.make_async_copy(ref, ref, a_sem.at[sem]).wait()

    own_a.wait()
    send_a_rows(own, 0, 1, to_right).start()
    send_a_rows(own, 1, 4, to_left).start()
    send_a_rows(own, 1, 2, to_right).start()
    send_a_rows(own, 0, 3, to_left).start()
    send_a_block(own, 0, to_core).start()

    def wait_w(slot, part):
        ref = w_buf.at[slot * 2 + (xl + part) % 2]
        pltpu.make_async_copy(ref, ref, w_sem.at[slot * 2 + part]).wait()

    def send_w(slot, part, to_slot, to):
        row = (xl + part) % 2
        remote(
            w_buf.at[slot * 2 + row],
            w_buf.at[to_slot * 2 + row],
            w_send,
            w_sem.at[to_slot * 2 + part],
            to,
        ).start()

    def forward(slot, part, to_slot, to):
        wait_w(slot, part)
        send_w(slot, part, to_slot, to)

    def multiply(xh_of, slots):
        total = None
        for k in range(2):
            rows = a_buf[pl.ds(k * 4 + xh_of * 2, 2)].reshape(2 * LEN, KB)
            cols = [w_buf[slot * 2 + k] for slot in slots]
            cols = cols[0] if len(cols) == 1 else jnp.concatenate(cols, axis=1)
            part = dot32(rows, cols, NN_DIMS)
            total = part if total is None else total + part
        for i, slot in enumerate(slots):
            p_buf[pl.ds(slot * 4 + xh_of * 2, 2)] = (
                total[:, i * 128 : (i + 1) * 128].astype(BF16).reshape(2, LEN, 128)
            )
        send_partials(xh_of, slots)

    offset = {0: 0, 1: 7, 2: 1, 3: 6, 4: 2, 5: 5, 6: 3, 7: 4}

    def send_partials(xh_of, slots):
        side = (xh_of + xh) % 2
        for slot in slots:
            owner = (z + offset[slot]) % NZ
            y_to = owner // 2
            group = (owner % 2) * 2 + xh_of
            away = (y_to - y + NY) % NY
            via = (y + 1 + 2 * side) % NY
            for c_of in range(2):
                src = p_buf.at[slot * 4 + xh_of * 2 + c_of]

                @pl.when((away == 0) & (c_of == c))
                def _():
                    pltpu.make_async_copy(src, r_buf.at[group, c], r_sem.at[group, c]).start()

                @pl.when((away == 0) & (c_of != c))
                def _():
                    remote(src, r_buf.at[group, c], p_send, r_sem.at[group, c], to_core).start()

                @pl.when(away == 2)
                def _():
                    index = (side * 2 + owner % 2) * 2 + c_of
                    remote(
                        src, f_buf.at[index], p_send, f_sem.at[index], dev(z, via, x, c)
                    ).start()

                @pl.when(away == 3 - 2 * side)
                def _():
                    place = 2 * (1 + away // 3) + c
                    remote(
                        src,
                        r_buf.at[group, place],
                        p_send,
                        r_sem.at[group, place],
                        dev(z, y_to, x, c_of),
                    ).start()

    def pass_sums(xh_of, slots):
        side = (xh_of + xh) % 2
        for slot in slots:
            owner = (z + offset[slot]) % NZ
            y_to = owner // 2
            group = (owner % 2) * 2 + xh_of
            away = (y_to - y + NY) % NY

            @pl.when(away == 1 + 2 * side)
            def _():
                for c_of in range(2):
                    index = (side * 2 + owner % 2) * 2 + c_of
                    wait_copy(f_buf.at[index], f_sem.at[index])
                    f_buf[index] = (
                        f_buf[index].astype(F32)
                        + p_buf[slot * 4 + xh_of * 2 + c_of].astype(F32)
                    ).astype(BF16)
                    place = 2 * (1 + away // 3) + c
                    remote(
                        f_buf.at[index],
                        r_buf.at[group, place],
                        p_send,
                        r_sem.at[group, place],
                        dev(z, y_to, x, c_of),
                    ).start()

    wait_w(0, 0)
    send_w(0, 0, 1, to_up)
    send_w(0, 0, 2, to_down)
    early_send[0:RANK] = dot32(down_ref[...], a_buf[own], NT_DIMS)
    wait_w(0, 1)
    send_w(0, 1, 1, to_up)
    send_w(0, 1, 2, to_down)
    load_up.wait()
    load_res.wait()
    load_dlt.wait()
    early_send[RANK : 2 * RANK] = dot32(up_buf[...], res_buf[...], NT_DIMS) + dot32(
        up_buf[...], dlt_buf[...], NT_DIMS
    )
    forward(1, 0, 3, to_up)
    forward(2, 0, 4, to_down)
    ones = jnp.ones((8, 128), F32)
    acc_buf[0] = jnp.zeros((LEN, 128), F32)
    for j in range(8):
        cols = pl.ds(j * 128, 128)
        target = res_buf[:, cols].astype(F32) + dlt_buf[:, cols].astype(F32)
        acc_buf[0] += target * target
    early_send[2 * RANK :] = dot_high(ones, acc_buf[0], NT_DIMS)
    for step in range(1, NT):
        remote(
            early_send, early_recv.at[t], small_send.at[0], early_sem.at[t], (dp, (t + step) % NT)
        ).start()
    pltpu.make_async_copy(early_send, early_recv.at[t], early_sem.at[t]).start()
    far = (x + 2) % NX
    wait_a_rows(a_index(left, c), 0, 1)
    send_a_rows(a_index(left, c), 0, 5, to_right).start()
    wait_a_rows(a_index(right, c), 1, 4)
    send_a_rows(a_index(right, c), 1, 6, to_left).start()
    forward(1, 1, 3, to_up)
    forward(2, 1, 4, to_down)
    wait_a_rows(a_index(left, c), 1, 2)
    send_a_block(a_index(left, c), 7, to_core).start()
    wait_a_rows(a_index(right, c), 0, 3)
    send_a_block(a_index(right, c), 8, to_core).start()
    forward(3, 0, 5, to_up)
    forward(4, 0, 6, to_down)
    wait_a_block(a_index(x, 1 - c), 0)
    wait_a_block(a_index(left, 1 - c), 7)
    wait_a_block(a_index(right, 1 - c), 8)
    multiply(xh, (0,))
    multiply(xh, (1, 2))
    forward(3, 1, 5, to_up)
    forward(4, 1, 6, to_down)
    multiply(xh, (3, 4))
    wait_a_rows(a_index(far, c), 0, 5)
    wait_a_rows(a_index(far, c), 1, 6)
    send_a_block(a_index(far, c), 9, to_core).start()
    forward(5, 0, 7, to_up)
    wait_w(6, 0)
    wait_a_block(a_index(far, 1 - c), 9)
    multiply(1 - xh, (0,))
    multiply(1 - xh, (1, 2))
    multiply(1 - xh, (3, 4))
    wait_w(5, 1)
    forward(6, 1, 7, to_down)
    multiply(1 - xh, (5, 6))
    multiply(xh, (5, 6))
    pass_sums(xh, (0,))
    pass_sums(xh, (1, 2))
    pass_sums(xh, (3, 4))
    wait_w(7, 0)
    wait_w(7, 1)
    multiply(1 - xh, (7,))
    multiply(xh, (7,))
    pass_sums(1 - xh, (0,))
    pass_sums(1 - xh, (1, 2))
    pass_sums(1 - xh, (3, 4))
    pass_sums(1 - xh, (5, 6))
    pass_sums(xh, (5, 6))
    pass_sums(1 - xh, (7,))
    pass_sums(xh, (7,))

    for turn in (2, 1, 3, 0):
        x_to = (x + turn) % NX
        group = (x_to % 2) * 2 + x_to // 2
        for source in range(6):
            wait_copy(r_buf.at[group, source], r_sem.at[group, source])
        for c_of in range(2):
            total = r_buf[group, c_of].astype(F32)
            for place in range(1, 3):
                total = total + r_buf[group, place * 2 + c_of].astype(F32)
            xs_buf[x_to, c_of] = total.astype(BF16)
        if turn == 0:
            pltpu.make_async_copy(xs_buf.at[x_to], xr_buf.at[x], x_sem.at[x]).start()
        else:
            remote(
                xs_buf.at[x_to], xr_buf.at[x], x_send, x_sem.at[x], dev(z, y, x_to, c)
            ).start()

    wait_all(early_recv, early_sem, NT)
    early = early_recv[0]
    for other in range(1, NT):
        early = early + early_recv[other]
    low_rank = early[0:RANK]
    target_up = early[RANK : 2 * RANK]
    sq_target = early[2 * RANK : 2 * RANK + 1]
    low3 = split3(2.0 * low_rank)

    for i in range(3):
        acc_buf[i] = jnp.zeros((LEN, 128), F32)
    for turn in (0, 1, 3, 2):
        x_of = (x + turn) % NX
        wait_copy(xr_buf.at[x_of], x_sem.at[x_of])
        for c_of in range(2):
            start = ((x_of // 2) * 4 + c_of * 2 + x_of % 2) * 128
            cols = pl.ds(pl.multiple_of(start, 128), 128)
            up3 = jnp.concatenate([up_buf[:, cols]] * 3, axis=0)
            res = res_buf[:, cols].astype(F32)
            state = res + xr_buf[x_of, c_of].astype(F32) + dot32(low3, up3, TN_DIMS)
            ad_buf[:, cols] = state.astype(BF16)
            target = res + dlt_buf[:, cols].astype(F32)
            gap = state - target
            acc_buf[0] += state * state
            acc_buf[1] += state * target
            acc_buf[2] += gap * gap
            high = gap.astype(BF16)
            ghi_buf[:, cols] = high
            glo_buf[:, cols] = (gap - high.astype(F32)).astype(BF16)
    store_adapted = pltpu.make_async_copy(ad_buf, adapted_hbm, out_sem)
    store_adapted.start()
    late_send[0:RANK] = dot32(up_buf[...], ghi_buf[...], NT_DIMS) + dot32(
        up_buf[...], glo_buf[...], NT_DIMS
    )
    row = lax.broadcasted_iota(jnp.int32, (8, 128), 0)
    stats = None
    for i in range(3):
        part = dot_high((row == i).astype(F32), acc_buf[i], NT_DIMS)
        stats = part if stats is None else stats + part
    late_send[RANK:] = stats
    for step in range(1, NT):
        remote(
            late_send, late_recv.at[t], small_send.at[1], late_sem.at[t], (dp, (t + step) % NT)
        ).start()
    pltpu.make_async_copy(late_send, late_recv.at[t], late_sem.at[t]).start()

    rank = lax.broadcasted_iota(jnp.int32, (1, NDP), 1)

    def total_and_here(count_ref):
        count = count_ref[...].astype(F32)
        here = jnp.where(rank == dp, count, 0.0)
        return jnp.sum(count, axis=1, keepdims=True), jnp.sum(here, axis=1, keepdims=True)

    harm_sum, harm_here = total_and_here(harm_ref)
    keep_sum, keep_here = total_and_here(keep_ref)
    position = lax.broadcasted_iota(jnp.int32, (1, LEN), 1).astype(F32)
    harmful = (position < harm_here).astype(F32)
    retained = ((position >= harm_here) & (position < harm_here + keep_here)).astype(F32)
    weight_harm = REROUTE_WEIGHT / harm_sum * harmful
    weight_keep = RETAIN_WEIGHT / keep_sum * retained

    wait_all(late_recv, late_sem, NT)
    late = late_recv[0]
    for other in range(1, NT):
        late = late + late_recv[other]
    gap_up = late[0:RANK]
    norm_h = jnp.sqrt(late[RANK : RANK + 1] + NORM_EPS)
    cross = late[RANK + 1 : RANK + 2]
    distance = jnp.sqrt(late[RANK + 2 : RANK + 3] + NORM_EPS)
    norm_g = jnp.sqrt(sq_target + NORM_EPS)
    cosine = cross / (norm_h * norm_g)
    first = weight_harm / (norm_h * norm_g)
    second = weight_harm * cosine / (norm_h * norm_h)
    third = weight_keep / distance
    by_target = 2.0 * (first - second)
    by_gap = 2.0 * (third - second)
    low_cot = by_target * target_up + by_gap * gap_up
    ga = fold3(dot32(split3(low_cot), a_buf[own], NN_DIMS))
    left_side = split3(low_rank * by_target)
    right_side = split3(low_rank * by_gap)
    gb = fold3(
        dot32(left_side, res_buf[...], NN_DIMS)
        + dot32(left_side, dlt_buf[...], NN_DIMS)
        + dot32(right_side, ghi_buf[...], NN_DIMS)
        + dot32(right_side, glo_buf[...], NN_DIMS)
    )
    for j in range(8):
        g_send[0:RANK, j, :] = ga[:, j * 128 : (j + 1) * 128]
        g_send[RANK:, j, :] = gb[:, j * 128 : (j + 1) * 128]

    @pl.loop(1, NDP)
    def _(step):
        to = (dp + step) % NDP
        remote(g_send.at[to], g_recv.at[dp], small_send.at[2], g_sem.at[dp], (to, t)).start()

    pltpu.make_async_copy(g_send.at[dp], g_recv.at[dp], g_sem.at[dp]).start()
    wait_all(g_recv, g_sem, NDP)
    total = g_recv[0]
    for other in range(1, NDP):
        total = total + g_recv[other]
    h_send[...] = total

    @pl.loop(1, NDP)
    def _(step):
        remote(
            h_send, h_recv.at[dp], small_send.at[3], h_sem.at[dp], ((dp + step) % NDP, t)
        ).start()

    pltpu.make_async_copy(h_send, h_recv.at[dp], h_sem.at[dp]).start()
    wait_all(h_recv, h_sem, NDP)
    for step in range(1, NT):
        remote(
            h_recv.at[pl.ds(RANK + 8 * c, 8)],
            b_recv.at[t, c],
            small_send.at[4],
            b_sem.at[t, 0],
            (dp, (t + step) % NT),
        ).start()
    for half in range(2):
        pltpu.make_async_copy(
            h_recv.at[pl.ds(RANK + 8 * half, 8)], b_recv.at[t, half], b_sem.at[t, half]
        ).start()
    for j in range(8):
        ga_ref[:, j * 128 : (j + 1) * 128] = h_recv[0:RANK, j, :]
    for step in range(1, NT):
        source = (t + step) % NT
        wait_copy(b_recv.at[source, c], b_sem.at[source, 0])
        remote(
            b_recv.at[source, c],
            b_recv.at[source, c],
            small_send.at[4],
            b_sem.at[source, 1],
            to_core,
        ).start()
    wait_copy(b_recv.at[t, 0], b_sem.at[t, 0])
    wait_copy(b_recv.at[t, 1], b_sem.at[t, 1])
    for step in range(1, NT):
        source = (t + step) % NT
        wait_copy(b_recv.at[source, 1 - c], b_sem.at[source, 1])
    for t_of in range(NT):
        for j in range(8):
            start = t_of * KB + j * 128
            gb_ref[0:8, start : start + 128] = b_recv[t_of, 0, :, j, :]
            gb_ref[8:16, start : start + 128] = b_recv[t_of, 1, :, j, :]

    wait_copy(a_buf.at[pl.ds(0, 7)], a_send)
    wait_copy(w_buf.at[pl.ds(0, 15)], w_send)
    wait_copy(p_buf.at[pl.ds(0, 28)], p_send)
    wait_copy(xs_buf.at[pl.ds(0, 3)], x_send)
    wait_copy(early_recv.at[pl.ds(0, NT - 1)], small_send.at[0])
    wait_copy(late_recv.at[pl.ds(0, NT - 1)], small_send.at[1])
    wait_copy(g_recv.at[pl.ds(0, NDP - 1)], small_send.at[2])
    wait_copy(h_recv.at[pl.ds(0, NDP - 1)], small_send.at[3])
    wait_copy(b_recv.at[pl.ds(0, NT - 1)], small_send.at[4])
    store_adapted.wait()


def local(ctx, w, down, up, res, dlt, harm, keep):
    vmem = pl.BlockSpec(memory_space=pltpu.VMEM)
    anyw = pl.BlockSpec(memory_space=pl.ANY)
    adapted, ga, gb = pl.pallas_call(
        kernel,
        out_shape=(
            jax.ShapeDtypeStruct((LEN, KB), BF16),
            jax.ShapeDtypeStruct((RANK, KB), F32),
            jax.ShapeDtypeStruct((RANK, NT * KB), F32),
        ),
        in_specs=[anyw, anyw, vmem, anyw, anyw, anyw, vmem, vmem],
        out_specs=(anyw, vmem, vmem),
        scratch_shapes=[
            pltpu.VMEM((8, LEN, KB), BF16),
            pltpu.VMEM((16, KB, 128), BF16),
            pltpu.VMEM((32, LEN, 128), BF16),
            pltpu.VMEM((4, 6, LEN, 128), BF16),
            pltpu.VMEM((8, LEN, 128), BF16),
            pltpu.VMEM((4, 2, LEN, 128), BF16),
            pltpu.VMEM((4, 2, LEN, 128), BF16),
            pltpu.VMEM((RANK, KB), BF16),
            pltpu.VMEM((LEN, KB), BF16),
            pltpu.VMEM((LEN, KB), BF16),
            pltpu.VMEM((LEN, KB), BF16),
            pltpu.VMEM((LEN, KB), BF16),
            pltpu.VMEM((LEN, KB), BF16),
            pltpu.VMEM((40, LEN), F32),
            pltpu.VMEM((NT, 40, LEN), F32),
            pltpu.VMEM((24, LEN), F32),
            pltpu.VMEM((NT, 24, LEN), F32),
            pltpu.VMEM((NDP, 8, 128), F32),
            pltpu.VMEM((NDP, 8, 128), F32),
            pltpu.VMEM((8, 128), F32),
            pltpu.VMEM((NDP, 8, 128), F32),
            pltpu.VMEM((NT, 2, 8, 8, 128), F32),
            pltpu.VMEM((3, LEN, 128), F32),
            pltpu.SemaphoreType.DMA((4,)),
            pltpu.SemaphoreType.DMA,
            pltpu.SemaphoreType.DMA,
            pltpu.SemaphoreType.DMA((10,)),
            pltpu.SemaphoreType.DMA,
            pltpu.SemaphoreType.DMA((16,)),
            pltpu.SemaphoreType.DMA,
            pltpu.SemaphoreType.DMA((4, 6)),
            pltpu.SemaphoreType.DMA((8,)),
            pltpu.SemaphoreType.DMA,
            pltpu.SemaphoreType.DMA((NX,)),
            pltpu.SemaphoreType.DMA((5,)),
            pltpu.SemaphoreType.DMA((NT,)),
            pltpu.SemaphoreType.DMA((NT,)),
            pltpu.SemaphoreType.DMA((NDP,)),
            pltpu.SemaphoreType.DMA((NDP,)),
            pltpu.SemaphoreType.DMA((NT, 2)),
        ],
        compiler_params=pltpu.CompilerParams(
            collective_id=0, has_side_effects=True, vmem_limit_bytes=56 * 1024 * 1024
        ),
    )(ctx, w, down.T, up, res, dlt, harm.reshape(1, NDP), keep.reshape(1, NDP))
    return adapted, ga.T, gb


def solution(mesh):
    return jax.shard_map(
        local,
        mesh=mesh,
        in_specs=(
            P("dp", "tensor"),
            P("tensor", "dp"),
            P("tensor", None),
            P(),
            P("dp", "tensor"),
            P("dp", "tensor"),
            P(),
            P(),
        ),
        out_specs=(P("dp", "tensor"), P("tensor", None), P()),
        check_vma=False,
    )
```

```python
import jax
import jax.numpy as jnp
from jax import lax
from jax.experimental import pallas as pl
from jax.experimental.pallas import tpu as pltpu
from jax.sharding import PartitionSpec as P

NORM_EPS = 1e-06
REROUTE_WEIGHT = 65536.0
RETAIN_WEIGHT = 1024.0

NZ = 8
NY = 4
NX = 4
NT = 8
NDP = 32
LEN = 384
HALF = LEN // 2
KB = 1024
RANK = 16
F32 = jnp.float32
BF16 = jnp.bfloat16
NT_DIMS = (((1,), (1,)), ((), ()))
TN_DIMS = (((0,), (0,)), ((), ()))
NN_DIMS = (((1,), (0,)), ((), ()))


def split3(value):
    hi = value.astype(BF16)
    rest = value - hi.astype(F32)
    mid = rest.astype(BF16)
    low = (rest - mid.astype(F32)).astype(BF16)
    return jnp.concatenate([hi, mid, low], axis=0)


def fold3(value):
    return value[0:RANK] + value[RANK : 2 * RANK] + value[2 * RANK : 3 * RANK]


def dot32(a, b, dims):
    return lax.dot_general(a, b, dims, preferred_element_type=F32)


def dot_high(a, b, dims):
    return lax.dot_general(a, b, dims, precision=lax.Precision.HIGHEST, preferred_element_type=F32)


def kernel(
    ctx_hbm,
    w_hbm,
    down_ref,
    up_hbm,
    res_hbm,
    dlt_hbm,
    harm_ref,
    keep_ref,
    adapted_hbm,
    ga_ref,
    gb_ref,
    a_buf,
    w_buf,
    p_buf,
    r_buf,
    f_buf,
    xs_buf,
    xr_buf,
    up_buf,
    res_buf,
    dlt_buf,
    ad_buf,
    ghi_buf,
    glo_buf,
    early_send,
    early_recv,
    late_send,
    late_recv,
    g_send,
    g_recv,
    h_send,
    h_recv,
    b_recv,
    acc_buf,
    in_sem,
    out_sem,
    a_send,
    a_sem,
    w_send,
    w_sem,
    p_send,
    r_sem,
    f_sem,
    x_send,
    x_sem,
    small_send,
    early_sem,
    late_sem,
    g_sem,
    h_sem,
    b_sem,
):
    dp = lax.axis_index("dp")
    t = lax.axis_index("tensor")
    z = dp // 4
    xh = (dp // 2) % 2
    c = dp % 2
    y = t // 2
    xl = t % 2
    x = 2 * xh + xl
    right = (x + 1) % NX
    left = (x + 3) % NX

    def dev(z_to, y_to, x_to, c_to):
        return (z_to * 4 + (x_to // 2) * 2 + c_to, y_to * 2 + x_to % 2)

    def remote(src, dst, send, recv, to):
        return pltpu.make_async_remote_copy(
            src_ref=src,
            dst_ref=dst,
            send_sem=send,
            recv_sem=recv,
            device_id=to,
            device_id_type=pl.DeviceIdType.MESH,
        )

    def wait_copy(ref, sem):
        pltpu.make_async_copy(ref, ref, sem).wait()

    def wait_all(ref, sems, count):
        @pl.loop(0, count)
        def _(source):
            wait_copy(ref.at[source], sems.at[source])

    to_right = dev(z, y, right, c)
    to_left = dev(z, y, left, c)
    to_core = dev(z, y, x, 1 - c)
    to_pair = dev(z, y, 2 * xh + (1 - xl), c)
    to_up = dev((z + 1) % NZ, y, x, c)
    to_down = dev((z + 7) % NZ, y, x, c)

    def a_index(x_of, c_of):
        return (x_of % 2) * 4 + (x_of // 2) * 2 + c_of

    own = a_index(x, c)
    own_a = pltpu.make_async_copy(ctx_hbm, a_buf.at[own], in_sem.at[0])
    own_a.start()
    own_w = pltpu.make_async_copy(
        w_hbm.at[:, pl.ds(pl.multiple_of(xl * 128, 128), 128)], w_buf.at[xl], w_sem.at[0]
    )
    own_w.start()
    load_up = pltpu.make_async_copy(
        up_hbm.at[:, pl.ds(pl.multiple_of(t * KB, KB), KB)], up_buf, in_sem.at[1]
    )
    load_up.start()
    load_res = pltpu.make_async_copy(res_hbm, res_buf, in_sem.at[2])
    load_res.start()
    load_dlt = pltpu.make_async_copy(dlt_hbm, dlt_buf, in_sem.at[3])
    load_dlt.start()

    barrier = pltpu.get_barrier_semaphore()

    def greet(to):
        pl.semaphore_signal(barrier, inc=1, device_id=to, device_id_type=pl.DeviceIdType.MESH)

    for step in range(1, NY):
        greet(dev(z, (y + step) % NY, x, 1 - c))
    for step in range(1, NT):
        greet((dp, (t + step) % NT))
    for near in (
        to_core,
        to_up,
        to_down,
        dev(z, y, 2 * (1 - xh) + (1 - xl), c),
        dev(z, y, 2 * (1 - xh) + xl, c),
        dev(z, y, 2 * (1 - xh) + xl, 1 - c),
    ):
        greet(near)
    pl.semaphore_wait(barrier, (NY - 1) + (NT - 1) + 6)

    send_pair = remote(
        w_hbm.at[:, pl.ds(pl.multiple_of((1 - xl) * 128, 128), 128)],
        w_buf.at[xl],
        w_send,
        w_sem.at[1],
        to_pair,
    )
    send_pair.start()

    def send_a_rows(block, rows, sem, to):
        return remote(
            a_buf.at[block, pl.ds(rows * HALF, HALF)],
            a_buf.at[block, pl.ds(rows * HALF, HALF)],
            a_send,
            a_sem.at[sem],
            to,
        )

    def send_a_block(block, sem, to):
        return remote(a_buf.at[block], a_buf.at[block], a_send, a_sem.at[sem], to)

    def wait_a_rows(block, rows, sem):
        ref = a_buf.at[block, pl.ds(rows * HALF, HALF)]
        pltpu.make_async_copy(ref, ref, a_sem.at[sem]).wait()

    def wait_a_block(block, sem):
        ref = a_buf.at[block]
        pltpu.make_async_copy(ref, ref, a_sem.at[sem]).wait()

    own_a.wait()
    send_a_rows(own, 0, 1, to_right).start()
    send_a_rows(own, 1, 4, to_left).start()
    send_a_rows(own, 1, 2, to_right).start()
    send_a_rows(own, 0, 3, to_left).start()
    send_a_block(own, 0, to_core).start()

    def wait_w(slot, part):
        ref = w_buf.at[slot * 2 + (xl + part) % 2]
        pltpu.make_async_copy(ref, ref, w_sem.at[slot * 2 + part]).wait()

    def send_w(slot, part, to_slot, to):
        row = (xl + part) % 2
        remote(
            w_buf.at[slot * 2 + row],
            w_buf.at[to_slot * 2 + row],
            w_send,
            w_sem.at[to_slot * 2 + part],
            to,
        ).start()

    def forward(slot, part, to_slot, to):
        wait_w(slot, part)
        send_w(slot, part, to_slot, to)

    def multiply(xh_of, slots):
        total = None
        for k in range(2):
            rows = a_buf[pl.ds(k * 4 + xh_of * 2, 2)].reshape(2 * LEN, KB)
            cols = [w_buf[slot * 2 + k] for slot in slots]
            cols = cols[0] if len(cols) == 1 else jnp.concatenate(cols, axis=1)
            part = dot32(rows, cols, NN_DIMS)
            total = part if total is None else total + part
        for i, slot in enumerate(slots):
            p_buf[pl.ds(slot * 4 + xh_of * 2, 2)] = (
                total[:, i * 128 : (i + 1) * 128].astype(BF16).reshape(2, LEN, 128)
            )
        send_partials(xh_of, slots)

    offset = {0: 0, 1: 7, 2: 1, 3: 6, 4: 2, 5: 5, 6: 3, 7: 4}

    def send_partials(xh_of, slots):
        side = (xh_of + xh) % 2
        for slot in slots:
            owner = (z + offset[slot]) % NZ
            y_to = owner // 2
            group = (owner % 2) * 2 + xh_of
            away = (y_to - y + NY) % NY
            via = (y + 1 + 2 * side) % NY
            for c_of in range(2):
                src = p_buf.at[slot * 4 + xh_of * 2 + c_of]

                @pl.when((away == 0) & (c_of == c))
                def _():
                    pltpu.make_async_copy(src, r_buf.at[group, c], r_sem.at[group, c]).start()

                @pl.when((away == 0) & (c_of != c))
                def _():
                    remote(src, r_buf.at[group, c], p_send, r_sem.at[group, c], to_core).start()

                @pl.when(away == 2)
                def _():
                    index = (side * 2 + owner % 2) * 2 + c_of
                    remote(
                        src, f_buf.at[index], p_send, f_sem.at[index], dev(z, via, x, c)
                    ).start()

                @pl.when(away == 3 - 2 * side)
                def _():
                    place = 2 * (1 + away // 3) + c
                    remote(
                        src,
                        r_buf.at[group, place],
                        p_send,
                        r_sem.at[group, place],
                        dev(z, y_to, x, c_of),
                    ).start()

    def pass_sums(xh_of, slots):
        side = (xh_of + xh) % 2
        for slot in slots:
            owner = (z + offset[slot]) % NZ
            y_to = owner // 2
            group = (owner % 2) * 2 + xh_of
            away = (y_to - y + NY) % NY

            @pl.when(away == 1 + 2 * side)
            def _():
                for c_of in range(2):
                    index = (side * 2 + owner % 2) * 2 + c_of
                    wait_copy(f_buf.at[index], f_sem.at[index])
                    f_buf[index] = (
                        f_buf[index].astype(F32)
                        + p_buf[slot * 4 + xh_of * 2 + c_of].astype(F32)
                    ).astype(BF16)
                    place = 2 * (1 + away // 3) + c
                    remote(
                        f_buf.at[index],
                        r_buf.at[group, place],
                        p_send,
                        r_sem.at[group, place],
                        dev(z, y_to, x, c_of),
                    ).start()

    wait_w(0, 0)
    send_w(0, 0, 1, to_up)
    send_w(0, 0, 2, to_down)
    early_send[0:RANK] = dot32(down_ref[...], a_buf[own], NT_DIMS)
    wait_w(0, 1)
    send_w(0, 1, 1, to_up)
    send_w(0, 1, 2, to_down)
    load_up.wait()
    load_res.wait()
    load_dlt.wait()
    early_send[RANK : 2 * RANK] = dot32(up_buf[...], res_buf[...], NT_DIMS) + dot32(
        up_buf[...], dlt_buf[...], NT_DIMS
    )
    forward(1, 0, 3, to_up)
    forward(2, 0, 4, to_down)
    row = lax.broadcasted_iota(jnp.int32, (8, 128), 0)
    acc_buf[0] = jnp.zeros((LEN, 128), F32)
    for j in range(8):
        cols = pl.ds(j * 128, 128)
        target = res_buf[:, cols].astype(F32) + dlt_buf[:, cols].astype(F32)
        acc_buf[0] += target * target
    target_stats = dot_high((row == 3).astype(F32), acc_buf[0], NT_DIMS)
    for step in range(1, NT):
        remote(
            early_send, early_recv.at[t], small_send.at[0], early_sem.at[t], (dp, (t + step) % NT)
        ).start()
    pltpu.make_async_copy(early_send, early_recv.at[t], early_sem.at[t]).start()
    far = (x + 2) % NX
    wait_a_rows(a_index(left, c), 0, 1)
    send_a_rows(a_index(left, c), 0, 5, to_right).start()
    wait_a_rows(a_index(right, c), 1, 4)
    send_a_rows(a_index(right, c), 1, 6, to_left).start()
    forward(1, 1, 3, to_up)
    forward(2, 1, 4, to_down)
    wait_a_rows(a_index(left, c), 1, 2)
    send_a_block(a_index(left, c), 7, to_core).start()
    wait_a_rows(a_index(right, c), 0, 3)
    send_a_block(a_index(right, c), 8, to_core).start()
    forward(3, 0, 5, to_up)
    forward(4, 0, 6, to_down)
    wait_a_block(a_index(x, 1 - c), 0)
    wait_a_block(a_index(left, 1 - c), 7)
    wait_a_block(a_index(right, 1 - c), 8)
    multiply(xh, (0,))
    multiply(xh, (1, 2))
    forward(3, 1, 5, to_up)
    forward(4, 1, 6, to_down)
    multiply(xh, (3, 4))
    wait_a_rows(a_index(far, c), 0, 5)
    wait_a_rows(a_index(far, c), 1, 6)
    send_a_block(a_index(far, c), 9, to_core).start()
    forward(5, 0, 7, to_up)
    wait_w(6, 0)
    wait_a_block(a_index(far, 1 - c), 9)
    multiply(1 - xh, (0,))
    multiply(1 - xh, (1, 2))
    multiply(1 - xh, (3, 4))
    wait_w(5, 1)
    forward(6, 1, 7, to_down)
    multiply(1 - xh, (5, 6))
    multiply(xh, (5, 6))
    pass_sums(xh, (0,))
    pass_sums(xh, (1, 2))
    pass_sums(xh, (3, 4))
    wait_w(7, 0)
    wait_w(7, 1)
    multiply(1 - xh, (7,))
    multiply(xh, (7,))
    pass_sums(1 - xh, (0,))
    pass_sums(1 - xh, (1, 2))
    pass_sums(1 - xh, (3, 4))
    pass_sums(1 - xh, (5, 6))
    pass_sums(xh, (5, 6))
    pass_sums(1 - xh, (7,))
    pass_sums(xh, (7,))

    for turn in (2, 1, 3, 0):
        x_to = (x + turn) % NX
        group = (x_to % 2) * 2 + x_to // 2
        for source in range(6):
            wait_copy(r_buf.at[group, source], r_sem.at[group, source])
        for c_of in range(2):
            total = r_buf[group, c_of].astype(F32)
            for place in range(1, 3):
                total = total + r_buf[group, place * 2 + c_of].astype(F32)
            xs_buf[x_to, c_of] = total.astype(BF16)
        if turn == 0:
            pltpu.make_async_copy(xs_buf.at[x_to], xr_buf.at[x], x_sem.at[x]).start()
        else:
            remote(
                xs_buf.at[x_to], xr_buf.at[x], x_send, x_sem.at[x], dev(z, y, x_to, c)
            ).start()

    wait_all(early_recv, early_sem, NT)
    early = early_recv[0]
    for other in range(1, NT):
        early = early + early_recv[other]
    low_rank = early[0:RANK]
    target_up = early[RANK : 2 * RANK]
    low3 = split3(2.0 * low_rank)

    for i in range(3):
        acc_buf[i] = jnp.zeros((LEN, 128), F32)
    for turn in (0, 1, 3, 2):
        x_of = (x + turn) % NX
        wait_copy(xr_buf.at[x_of], x_sem.at[x_of])
        for c_of in range(2):
            start = ((x_of // 2) * 4 + c_of * 2 + x_of % 2) * 128
            cols = pl.ds(pl.multiple_of(start, 128), 128)
            up3 = jnp.concatenate([up_buf[:, cols]] * 3, axis=0)
            res = res_buf[:, cols].astype(F32)
            state = res + xr_buf[x_of, c_of].astype(F32) + dot32(low3, up3, TN_DIMS)
            ad_buf[:, cols] = state.astype(BF16)
            target = res + dlt_buf[:, cols].astype(F32)
            gap = state - target
            acc_buf[0] += state * state
            acc_buf[1] += state * target
            acc_buf[2] += gap * gap
            high = gap.astype(BF16)
            ghi_buf[:, cols] = high
            glo_buf[:, cols] = (gap - high.astype(F32)).astype(BF16)
    store_adapted = pltpu.make_async_copy(ad_buf, adapted_hbm, out_sem)
    store_adapted.start()
    late_send[0:RANK] = dot32(up_buf[...], ghi_buf[...], NT_DIMS) + dot32(
        up_buf[...], glo_buf[...], NT_DIMS
    )
    stats = target_stats
    for i in range(3):
        stats = stats + dot_high((row == i).astype(F32), acc_buf[i], NT_DIMS)
    late_send[RANK:] = stats
    for step in range(1, NT):
        remote(
            late_send, late_recv.at[t], small_send.at[1], late_sem.at[t], (dp, (t + step) % NT)
        ).start()
    pltpu.make_async_copy(late_send, late_recv.at[t], late_sem.at[t]).start()

    rank = lax.broadcasted_iota(jnp.int32, (1, NDP), 1)

    def total_and_here(count_ref):
        count = count_ref[...].astype(F32)
        here = jnp.where(rank == dp, count, 0.0)
        return jnp.sum(count, axis=1, keepdims=True), jnp.sum(here, axis=1, keepdims=True)

    harm_sum, harm_here = total_and_here(harm_ref)
    keep_sum, keep_here = total_and_here(keep_ref)
    position = lax.broadcasted_iota(jnp.int32, (1, LEN), 1).astype(F32)
    harmful = (position < harm_here).astype(F32)
    retained = ((position >= harm_here) & (position < harm_here + keep_here)).astype(F32)
    weight_harm = REROUTE_WEIGHT / harm_sum * harmful
    weight_keep = RETAIN_WEIGHT / keep_sum * retained

    wait_all(late_recv, late_sem, NT)
    late = late_recv[0]
    for other in range(1, NT):
        late = late + late_recv[other]
    gap_up = late[0:RANK]
    norm_h = jnp.sqrt(late[RANK : RANK + 1] + NORM_EPS)
    cross = late[RANK + 1 : RANK + 2]
    distance = jnp.sqrt(late[RANK + 2 : RANK + 3] + NORM_EPS)
    norm_g = jnp.sqrt(late[RANK + 3 : RANK + 4] + NORM_EPS)
    cosine = cross / (norm_h * norm_g)
    first = weight_harm / (norm_h * norm_g)
    second = weight_harm * cosine / (norm_h * norm_h)
    third = weight_keep / distance
    by_target = 2.0 * (first - second)
    by_gap = 2.0 * (third - second)
    low_cot = by_target * target_up + by_gap * gap_up
    ga = fold3(dot32(split3(low_cot), a_buf[own], NN_DIMS))
    left_side = split3(low_rank * by_target)
    right_side = split3(low_rank * by_gap)
    gb = fold3(
        dot32(left_side, res_buf[...], NN_DIMS)
        + dot32(left_side, dlt_buf[...], NN_DIMS)
        + dot32(right_side, ghi_buf[...], NN_DIMS)
        + dot32(right_side, glo_buf[...], NN_DIMS)
    )
    for j in range(8):
        g_send[0:RANK, j, :] = ga[:, j * 128 : (j + 1) * 128]
        g_send[RANK:, j, :] = gb[:, j * 128 : (j + 1) * 128]

    @pl.loop(1, NDP)
    def _(step):
        to = (dp + step) % NDP
        remote(g_send.at[to], g_recv.at[dp], small_send.at[2], g_sem.at[dp], (to, t)).start()

    pltpu.make_async_copy(g_send.at[dp], g_recv.at[dp], g_sem.at[dp]).start()
    wait_all(g_recv, g_sem, NDP)
    total = g_recv[0]
    for other in range(1, NDP):
        total = total + g_recv[other]
    h_send[...] = total

    @pl.loop(1, NDP)
    def _(step):
        remote(
            h_send, h_recv.at[dp], small_send.at[3], h_sem.at[dp], ((dp + step) % NDP, t)
        ).start()

    pltpu.make_async_copy(h_send, h_recv.at[dp], h_sem.at[dp]).start()
    wait_all(h_recv, h_sem, NDP)
    for step in range(1, NT):
        remote(
            h_recv.at[pl.ds(RANK + 8 * c, 8)],
            b_recv.at[t, c],
            small_send.at[4],
            b_sem.at[t, 0],
            (dp, (t + step) % NT),
        ).start()
    for half in range(2):
        pltpu.make_async_copy(
            h_recv.at[pl.ds(RANK + 8 * half, 8)], b_recv.at[t, half], b_sem.at[t, half]
        ).start()
    for j in range(8):
        ga_ref[:, j * 128 : (j + 1) * 128] = h_recv[0:RANK, j, :]
    for step in range(1, NT):
        source = (t + step) % NT
        wait_copy(b_recv.at[source, c], b_sem.at[source, 0])
        remote(
            b_recv.at[source, c],
            b_recv.at[source, c],
            small_send.at[4],
            b_sem.at[source, 1],
            to_core,
        ).start()
    wait_copy(b_recv.at[t, 0], b_sem.at[t, 0])
    wait_copy(b_recv.at[t, 1], b_sem.at[t, 1])
    for step in range(1, NT):
        source = (t + step) % NT
        wait_copy(b_recv.at[source, 1 - c], b_sem.at[source, 1])
    for t_of in range(NT):
        for j in range(8):
            start = t_of * KB + j * 128
            gb_ref[0:8, start : start + 128] = b_recv[t_of, 0, :, j, :]
            gb_ref[8:16, start : start + 128] = b_recv[t_of, 1, :, j, :]

    wait_copy(a_buf.at[pl.ds(0, 7)], a_send)
    wait_copy(w_buf.at[pl.ds(0, 15)], w_send)
    wait_copy(p_buf.at[pl.ds(0, 28)], p_send)
    wait_copy(xs_buf.at[pl.ds(0, 3)], x_send)
    wait_copy(early_recv.at[pl.ds(0, NT - 1)], small_send.at[0])
    wait_copy(late_recv.at[pl.ds(0, NT - 1)], small_send.at[1])
    wait_copy(g_recv.at[pl.ds(0, NDP - 1)], small_send.at[2])
    wait_copy(h_recv.at[pl.ds(0, NDP - 1)], small_send.at[3])
    wait_copy(b_recv.at[pl.ds(0, NT - 1)], small_send.at[4])
    store_adapted.wait()


def local(ctx, w, down, up, res, dlt, harm, keep):
    vmem = pl.BlockSpec(memory_space=pltpu.VMEM)
    anyw = pl.BlockSpec(memory_space=pl.ANY)
    adapted, ga, gb = pl.pallas_call(
        kernel,
        out_shape=(
            jax.ShapeDtypeStruct((LEN, KB), BF16),
            jax.ShapeDtypeStruct((RANK, KB), F32),
            jax.ShapeDtypeStruct((RANK, NT * KB), F32),
        ),
        in_specs=[anyw, anyw, vmem, anyw, anyw, anyw, vmem, vmem],
        out_specs=(anyw, vmem, vmem),
        scratch_shapes=[
            pltpu.VMEM((8, LEN, KB), BF16),
            pltpu.VMEM((16, KB, 128), BF16),
            pltpu.VMEM((32, LEN, 128), BF16),
            pltpu.VMEM((4, 6, LEN, 128), BF16),
            pltpu.VMEM((8, LEN, 128), BF16),
            pltpu.VMEM((4, 2, LEN, 128), BF16),
            pltpu.VMEM((4, 2, LEN, 128), BF16),
            pltpu.VMEM((RANK, KB), BF16),
            pltpu.VMEM((LEN, KB), BF16),
            pltpu.VMEM((LEN, KB), BF16),
            pltpu.VMEM((LEN, KB), BF16),
            pltpu.VMEM((LEN, KB), BF16),
            pltpu.VMEM((LEN, KB), BF16),
            pltpu.VMEM((32, LEN), F32),
            pltpu.VMEM((NT, 32, LEN), F32),
            pltpu.VMEM((24, LEN), F32),
            pltpu.VMEM((NT, 24, LEN), F32),
            pltpu.VMEM((NDP, 8, 128), F32),
            pltpu.VMEM((NDP, 8, 128), F32),
            pltpu.VMEM((8, 128), F32),
            pltpu.VMEM((NDP, 8, 128), F32),
            pltpu.VMEM((NT, 2, 8, 8, 128), F32),
            pltpu.VMEM((3, LEN, 128), F32),
            pltpu.SemaphoreType.DMA((4,)),
            pltpu.SemaphoreType.DMA,
            pltpu.SemaphoreType.DMA,
            pltpu.SemaphoreType.DMA((10,)),
            pltpu.SemaphoreType.DMA,
            pltpu.SemaphoreType.DMA((16,)),
            pltpu.SemaphoreType.DMA,
            pltpu.SemaphoreType.DMA((4, 6)),
            pltpu.SemaphoreType.DMA((8,)),
            pltpu.SemaphoreType.DMA,
            pltpu.SemaphoreType.DMA((NX,)),
            pltpu.SemaphoreType.DMA((5,)),
            pltpu.SemaphoreType.DMA((NT,)),
            pltpu.SemaphoreType.DMA((NT,)),
            pltpu.SemaphoreType.DMA((NDP,)),
            pltpu.SemaphoreType.DMA((NDP,)),
            pltpu.SemaphoreType.DMA((NT, 2)),
        ],
        compiler_params=pltpu.CompilerParams(
            collective_id=0, has_side_effects=True, vmem_limit_bytes=56 * 1024 * 1024
        ),
    )(ctx, w, down.T, up, res, dlt, harm.reshape(1, NDP), keep.reshape(1, NDP))
    return adapted, ga.T, gb


def solution(mesh):
    return jax.shard_map(
        local,
        mesh=mesh,
        in_specs=(
            P("dp", "tensor"),
            P("tensor", "dp"),
            P("tensor", None),
            P(),
            P("dp", "tensor"),
            P("dp", "tensor"),
            P(),
            P(),
        ),
        out_specs=(P("dp", "tensor"), P("tensor", None), P()),
        check_vma=False,
    )
```
